32 devices in a mesh: seq: 8 (over z, y), dp: 4 (over x, core).
Axes of the slice: x: 2, y: 2, z: 4, core: 2. Of those that a mesh axis runs over, the one named last changes fastest.
Arguments:
- layer_in: bfloat16 [4, 2048, 768], P('dp', 'seq'), may hold values from -6 to 6
- out_grad: bfloat16 [4, 2048, 1536], P('dp', 'seq'), may hold values from -6 to 6
- x_weight: bfloat16 [768, 1536], replicated, may hold values from -0.21875 to 0.21875
- bc_weight: bfloat16 [768, 128], replicated, may hold values from -0.0390625 to 0.0390625
- dt_weight: bfloat16 [768, 24], replicated, may hold values from -0.21875 to 0.21875
- a_log: float32 [24], replicated, as said below
- dt_bias: float32 [24], replicated, may hold values from -1 to 1
- skip_gain: float32 [24], replicated, may hold values from 0.5 to 1.5
Outputs:
- grad_in: bfloat16 [4, 2048, 768], P('dp', 'seq')
- grad_x_weight: float32 [768, 1536], P(('seq', 'dp'))
- grad_bc_weight: float32 [768, 128], P(('seq', 'dp'))
- grad_dt_weight: float32 [768, 24], P(('seq', 'dp'))
- grad_a_log: float32 [24], replicated
- grad_dt_bias: float32 [24], replicated
- grad_skip: float32 [24], replicated
The draws below stay inside these ranges and needn't reach their ends.
Inputs may be any that keep to these rules, and one draw needn't show every extreme that they name: Each head's rate exp(a_log) is a positive number.
All inputs are finite; a program needn't handle non-finite values.
Results may differ from the reference program's by a relative error of at most 0.005.
Values sent between devices are 32-bit elements; how exact they have to be, the bound alone decides.
No kernel may reach another device: no remote copies, remote signals or barrier semaphores. Data moves between devices by JAX's collectives and lax.ppermute only.
A program may use at most 256 MiB of HBM per device.

```python
import math
import jax
import jax.numpy as jnp
from jax import lax

D = 768
INNER = 1536
STATE = 64
SPAN = 128
L_DEV = 256
HEADS = 24
SEQ_LEN = 2048
SEQS = 4
TOKENS = 8192
N_SEQ = 8


def draw_a_log(key, part):
    first, second, third = jax.random.split(key, 3)
    share = 0.5
    quick_heads = jax.random.uniform(first, (HEADS,)) < share
    slow_rates = jnp.log(jax.random.uniform(second, (HEADS,), minval=0.1, maxval=1.0) / SEQ_LEN)
    quick_rates = jnp.log(jax.random.uniform(third, (HEADS,), minval=1.0 / 60.0, maxval=1.0 / 20.0))
    return jnp.where(quick_heads, quick_rates, slow_rates).astype(jnp.float32)


def spiked(drawn, stream_key, source, target, shards_of, factor):
    def block_of(axis_at):
        return (jnp.arange(drawn.shape[axis_at]) // (drawn.shape[axis_at] // shards_of)).reshape((-1,) + (1,) * (drawn.ndim - 1 - axis_at))

    one_side = jax.random.permutation(stream_key, shards_of)[block_of(target)]
    second = (block_of(target) + shards_of // 2) % shards_of
    return jnp.where((block_of(source) == one_side) | (block_of(source) == second), factor * drawn, drawn)


def steps_of(own_key, extent, cuts, smallest, largest):
    factor_of = 1.0
    for position, blocks in cuts:
        steps = jax.random.uniform(jax.random.fold_in(jax.random.fold_in(own_key, 6), position), (blocks,), jnp.float32, smallest / len(cuts), largest / len(cuts))
        factor_of = factor_of * jnp.repeat(jnp.exp(steps), extent[position] // blocks).reshape((-1,) + (1,) * (len(extent) - 1 - position))
    return factor_of


def bell_draw(key, extent, scale, bound, shards=(), dtype=jnp.bfloat16):
    drawn = scale * jax.random.normal(key, extent, jnp.float32)
    if shards:
        drawn = drawn * steps_of(key, extent, shards, -0.22, 0.18)
    return jnp.clip(drawn, -bound, bound).astype(dtype)


def heavy_noise(stream_key, shape, scale, bound, pieces, heavy, kind=jnp.bfloat16):
    entries = scale * jax.random.normal(stream_key, shape, jnp.float32)
    if pieces:
        entries = entries * steps_of(stream_key, shape, pieces, -0.22, 0.18)
    return jnp.clip(spiked(entries, jax.random.fold_in(stream_key, 3), *heavy), -bound, bound).astype(kind)


def setup_inputs(seed: int = 0) -> dict:
    key_list = jax.random.split(jax.random.key(seed), 9)
    layer_in = heavy_noise(key_list[0], (SEQS, SEQ_LEN, D), 1.0, 6.0, ((0, 4), (1, 8)), (1, 2, 8, 2.0))
    out_grad = bell_draw(key_list[1], (SEQS, SEQ_LEN, INNER), 1.0, 6.0, ((0, 4), (1, 8)))
    x_weight = bell_draw(key_list[2], (D, INNER), D ** -0.5, 0.21875)
    bc_weight = bell_draw(key_list[3], (D, 2 * STATE), (D * SEQ_LEN // 64) ** -0.5, 0.0390625)
    dt_weight = bell_draw(key_list[4], (D, HEADS), D ** -0.5, 0.21875)
    a_log = draw_a_log(jax.random.fold_in(key_list[8], 71), 0)
    dt_bias = jnp.clip(jax.random.uniform(key_list[6], (HEADS,), jnp.float32, -1.0, 1.0), -1.0, 1.0)
    skip_gain = jnp.clip(jax.random.uniform(key_list[7], (HEADS,), jnp.float32, 0.5, 1.5), 0.5, 1.5)
    return {"layer_in": layer_in, "out_grad": out_grad, "x_weight": x_weight, "bc_weight": bc_weight, "dt_weight": dt_weight, "a_log": a_log, "dt_bias": dt_bias, "skip_gain": skip_gain}


HIGH = lax.Precision.HIGHEST

def pieces_of(projected, a_log, dt_bias, inner, state):
    heads = a_log.shape[0]
    count = projected.shape[0]
    values = projected[:, :inner].reshape(count, heads, inner // heads)
    b_part = projected[:, inner:inner + state]
    c_part = projected[:, inner + state:inner + 2 * state]
    step_size = jax.nn.softplus(projected[:, inner + 2 * state:] + dt_bias)
    log_decay = -jnp.exp(a_log) * step_size
    return (values, b_part, c_part, step_size, log_decay)

def span_output(carried, block, a_log, dt_bias, skip_gain, inner, state):
    values, b_part, c_part, step_size, log_decay = pieces_of(block, a_log, dt_bias, inner, state)
    cumulated = jnp.cumsum(log_decay, axis=0)
    count = values.shape[0]
    causal = (jnp.arange(count)[:, None] >= jnp.arange(count)[None, :])[None]
    spread = cumulated.T[:, :, None] - cumulated.T[:, None, :]
    masked = jnp.where(causal, spread, 0.0)
    scores = jnp.dot(c_part, b_part.T, precision=HIGH)
    mixing = jnp.where(causal, jnp.exp(masked), 0.0) * scores[None] * step_size.T[:, None, :]
    inside = jnp.einsum('hts,shp->thp', mixing, values, precision=HIGH)
    carried_part = jnp.exp(cumulated)[:, :, None] * jnp.einsum('tn,hpn->thp', c_part, carried, precision=HIGH)
    output = inside + carried_part + skip_gain[None, :, None] * values
    tail = jnp.exp(cumulated[-1][None, :] - cumulated) * step_size
    following = jnp.exp(cumulated[-1])[:, None, None] * carried + jnp.einsum('sh,shp,sn->hpn', tail, values, b_part, precision=HIGH)
    return (following, output.reshape(count, inner))

def span_state(carried, block, a_log, dt_bias, inner, state):
    values, b_part, c_part, step_size, log_decay = pieces_of(block, a_log, dt_bias, inner, state)
    cumulated = jnp.cumsum(log_decay, axis=0)
    tail = jnp.exp(cumulated[-1][None, :] - cumulated) * step_size
    return jnp.exp(cumulated[-1])[:, None, None] * carried + jnp.einsum('sh,shp,sn->hpn', tail, values, b_part, precision=HIGH)

def block_output(projected, a_log, dt_bias, skip_gain, entering, inner, state):
    count = projected.shape[0]
    spans = projected.reshape(count // SPAN, SPAN, projected.shape[1])

    def advance(carried, block):
        return span_output(carried, block, a_log, dt_bias, skip_gain, inner, state)
    _, outputs = lax.scan(advance, entering, spans)
    return outputs.reshape(count, inner)

def block_state(projected, a_log, dt_bias, inner, state):
    count = projected.shape[0]
    heads = a_log.shape[0]
    spans = projected.reshape(count // SPAN, SPAN, projected.shape[1])
    zero_state = jnp.zeros((heads, inner // heads, state), jnp.float32)

    def advance(carried, block):
        return (span_state(carried, block, a_log, dt_bias, inner, state), None)
    end_state, _ = lax.scan(advance, zero_state, spans)
    step_size = jax.nn.softplus(projected[:, inner + 2 * state:] + dt_bias)
    decay_total = lax.optimization_barrier(jnp.sum(-jnp.exp(a_log) * step_size, axis=0))
    return (decay_total, end_state)

def reference(layer_in, out_grad, x_weight, bc_weight, dt_weight, a_log, dt_bias, skip_gain):
    inner = x_weight.shape[1]
    state = bc_weight.shape[1] // 2
    heads = dt_weight.shape[1]
    head_size = inner // heads
    weights = jnp.concatenate([x_weight, bc_weight, dt_weight], axis=1)
    columns = weights.shape[1]
    inv_root = 1.0 / math.sqrt(TOKENS)
    zero_state = jnp.zeros((heads, head_size, state), jnp.float32)

    def one_sequence(pair):
        seq_in, seq_grad = pair
        projected = jnp.dot(seq_in, weights, preferred_element_type=jnp.float32).reshape(N_SEQ, L_DEV, columns)
        totals, ends = lax.map(lambda piece: block_state(piece, a_log, dt_bias, inner, state), projected)

        def forward(carry, item):
            return (jnp.exp(item[0])[:, None, None] * carry + item[1], carry)
        _, entering = lax.scan(forward, zero_state, (totals, ends))
        grad_blocks = seq_grad.astype(jnp.float32).reshape(N_SEQ, L_DEV, inner)

        def local_pull(item):
            piece, start_state, cotangent = item
            _, pull = jax.vjp(lambda a, b, c, d, e: block_output(a, b, c, d, e, inner, state), piece, a_log, dt_bias, skip_gain, start_state)
            return pull(cotangent)
        d_local, da_local, db_local, ds_local, lam = lax.map(local_pull, (projected, entering, grad_blocks))

        def backward(carry, item):
            return (item[1] + jnp.exp(item[0])[:, None, None] * carry, carry)
        _, adjoint = lax.scan(backward, zero_state, (totals, lam), reverse=True)
        total_grad = lax.optimization_barrier(jnp.sum(adjoint * jnp.exp(totals)[:, :, None, None] * entering, axis=(2, 3)))

        def state_pull(item):
            piece, decay_grad, state_grad = item
            _, pull = jax.vjp(lambda a, b, c: block_state(a, b, c, inner, state), piece, a_log, dt_bias)
            return pull((decay_grad, state_grad))
        d_carry, da_carry, db_carry = lax.map(state_pull, (projected, total_grad, adjoint))
        return (d_local.reshape(SEQ_LEN, columns), d_carry.reshape(SEQ_LEN, columns), lax.optimization_barrier(jnp.sum(da_local + da_carry, axis=0)), lax.optimization_barrier(jnp.sum(db_local + db_carry, axis=0)), lax.optimization_barrier(jnp.sum(ds_local, axis=0)))
    d_local, d_carry, da_all, db_all, ds_all = lax.map(one_sequence, (layer_in, out_grad))
    local_part, carry_part = lax.optimization_barrier((d_local.astype(jnp.bfloat16), d_carry.astype(jnp.bfloat16)))
    combined = (local_part.astype(jnp.float32) + carry_part.astype(jnp.float32)).reshape(TOKENS, columns)
    grad_flat = jnp.dot(combined, weights.astype(jnp.float32).T, precision=HIGH)
    grad_in = grad_flat.reshape(SEQS, SEQ_LEN, D).astype(jnp.bfloat16)
    grad_weights = jnp.dot(layer_in.reshape(TOKENS, D).astype(jnp.float32).T, combined, precision=HIGH) * inv_root
    return (grad_in, grad_weights[:, :inner], grad_weights[:, inner:inner + 2 * state], grad_weights[:, inner + 2 * state:], lax.optimization_barrier(jnp.sum(da_all, axis=0)) * inv_root, lax.optimization_barrier(jnp.sum(db_all, axis=0)) * inv_root, lax.optimization_barrier(jnp.sum(ds_all, axis=0)) * inv_root)
```

```python
import functools
import math

import jax
import jax.numpy as jnp
import numpy as np
from jax import lax
from jax.experimental import pallas as pl
from jax.experimental.pallas import tpu as pltpu
from jax.sharding import PartitionSpec as P

LANES = 128
HALF = 64
HIGH = lax.Precision.HIGHEST
F32 = jnp.float32
BF16 = jnp.bfloat16
COLOR_BLOCKS = (5, 4, 5)

NN = (((1,), (0,)), ((), ()))
NT = (((1,), (1,)), ((), ()))
TN = (((0,), (0,)), ((), ()))


def mm(a, b, dims=NN, precision=None):
    return lax.dot_general(a, b, dims, precision=precision, preferred_element_type=F32)


def iota(shape, axis):
    return lax.broadcasted_iota(jnp.int32, shape, axis)


def block(ref, j):
    return ref[:, j * LANES : (j + 1) * LANES]


def two_terms(f):
    hi = f.astype(BF16)
    lo = (f - hi.astype(F32)).astype(BF16)
    return jnp.concatenate([hi, lo], axis=1)


def three_terms(f):
    hi = f.astype(BF16)
    rest = f - hi.astype(F32)
    mid = rest.astype(BF16)
    lo = (rest - mid.astype(F32)).astype(BF16)
    return jnp.concatenate([hi, mid, lo], axis=1)


def spread_matrix(j, terms):
    row, lane = iota((LANES, LANES), 0), iota((LANES, LANES), 1)
    one = (row == 2 * j + lane // HALF).astype(F32).astype(BF16)
    return jnp.concatenate([one] * terms, axis=0)


def gather_matrix(j, dtype=BF16):
    row, lane = iota((LANES, LANES), 0), iota((LANES, LANES), 1)
    return (lane == 2 * j + row // HALF).astype(F32).astype(dtype)


def first_kernel(
    side_ref, in_ref, og_ref, xw_ref, bcw_ref, dtw_ref, alog_ref, bias_ref,
    x_out, bc_out, delta_out, cum_out, cumt_out, sig_out, xdw_out, dye_out,
    mine_out, send_out, pad,
):
    count, heads = in_ref.shape[0], dtw_ref.shape[1]
    inner = xw_ref.shape[1]
    blocks = inner // LANES
    lane = iota((1, LANES), 1)
    pad[...] = jnp.zeros_like(pad)
    pad[:count, :heads] = mm(in_ref[...], dtw_ref[...])
    pad[count : count + 1, :heads] = jnp.exp(alog_ref[...])
    pad[count + 1 : count + 2, :heads] = bias_ref[...]
    rate = pad[count : count + 1, :]
    pre = pad[:count, :] + pad[count + 1 : count + 2, :]
    small = jnp.exp(-jnp.abs(pre))
    delta = jnp.maximum(pre, 0.0) + jnp.log1p(small)
    sig_out[...] = jnp.where(pre >= 0.0, 1.0, small) / (1.0 + small)
    decay = -rate * delta
    lower = (iota((count, count), 0) >= iota((count, count), 1)).astype(F32)
    cum = mm(lower, decay, precision=HIGH)
    total = cum[count - 1 : count, :]
    delta_out[...] = delta
    cum_out[...] = cum
    cumt_out[...] = cum.T
    bc = mm(in_ref[...], bcw_ref[...])
    bc_out[...] = bc
    bc2 = two_terms(bc)
    tail = two_terms(delta * jnp.exp(total - cum))
    rise = two_terms(jnp.exp(cum))
    sums = three_terms(jnp.broadcast_to(total, (8, LANES)))
    first = side_ref[0] == 0
    half = blocks // 2
    e_parts, l_parts, g_parts = [], [], []
    for j in range(blocks):
        x = mm(in_ref[...], block(xw_ref, j))
        span = slice(j * LANES, (j + 1) * LANES)
        x_out[:, span] = x
        spread = spread_matrix(j, 2)
        xdw = (x * mm(tail, spread)).astype(BF16)
        dye = (block(og_ref, j).astype(F32) * mm(rise, spread)).astype(BF16)
        xdw_out[:, span] = xdw
        dye_out[:, span] = dye
        e_part, l_part = mm(bc2, xdw, TN), mm(bc2, dye, TN)
        e_parts.append(e_part[:HALF] + e_part[LANES : LANES + HALF])
        l_parts.append(l_part[HALF:LANES] + l_part[LANES + HALF :])
        g_parts.append(mm(sums, spread_matrix(j, 3)))
    for j in range(half):
        span = slice(j * LANES, (j + 1) * LANES)
        for n, parts in enumerate((e_parts, l_parts, g_parts)):
            low, high = parts[j], parts[j + half]
            rows = slice(n * HALF, n * HALF + low.shape[0])
            mine_out[rows, span] = jnp.where(first, low, high)
            send_out[rows, span] = jnp.where(first, high, low)


def turn_kernel(in_ref, src_ref, turned_out):
    width = in_ref.shape[1]
    for n in range(turned_out.shape[0]):
        chosen = (iota((width, width), 0) == src_ref[n : n + 1, :]).astype(F32).astype(BF16)
        turned_out[n] = mm(in_ref[...], chosen).T.astype(BF16)


def quad_kernel(
    base, og_ref, x_ref, bc_ref, delta_ref, cum_ref, cumt_ref,
    u_out, dcum_out, dbc_out, cumx, deltax, wsum, across, down, scores,
):
    count, part = og_ref.shape
    blocks = part // LANES
    lanes = iota((1, LANES), 1)
    low_lanes = lanes < HALF
    cum3, delta2 = three_terms(cum_ref[...]), two_terms(delta_ref[...])
    for j in range(blocks):
        cumx[:, j * LANES : (j + 1) * LANES] = mm(cum3, spread_matrix(base + j, 3))
        deltax[:, j * LANES : (j + 1) * LANES] = mm(delta2, spread_matrix(base + j, 2))
    bc = bc_ref[...]
    swapped = pltpu.roll(bc, HALF, 1)
    causal = iota((count, count), 1) >= iota((count, count), 0)
    scores[...] = jnp.where(causal, mm(jnp.where(low_lanes, bc, 0.0), swapped, NT, HIGH), 0.0)
    wsum[...] = jnp.zeros_like(wsum)
    across[...] = jnp.zeros_like(across)
    down[...] = jnp.zeros_like(down)
    starts = list(range(0, count, LANES))

    def pair(j, _):
        span = pl.ds(pl.multiple_of(j * LANES, LANES), LANES)
        og = og_ref[:, span].astype(F32)
        og_turned = pltpu.roll(og, HALF, 1)
        x = x_ref[:, span] * deltax[:, span]
        x_hi = x.astype(BF16).astype(F32)
        x_lo = pltpu.roll(x - x_hi, HALF, 1)
        cumj = cumx[:, span]
        outs = [None] * len(starts)
        for q in range(2):
            mine = low_lanes if q == 0 else jnp.logical_not(low_lanes)
            head = 2 * (base + j) + q
            xq = jnp.where(mine, x_hi, x_lo).astype(BF16)
            og_both = jnp.where(mine, og, og_turned).astype(BF16)
            ogq = jnp.where(mine, og, 0.0).astype(BF16)
            row = cumt_ref[pl.ds(head, 1), :]
            row_sum = jnp.zeros((1, count), F32)
            for n, s in enumerate(starts):
                rows = slice(s, s + LANES)
                d = mm(xq[rows], og_both[s:], NT)
                col = cumj[rows, q * HALF : q * HALF + 1]
                a = jnp.exp(jnp.minimum(row[:, s:] - col, 0.0))
                score = scores[rows, s:]
                w = a * d
                wsum[rows, s:] += w
                p = a * score
                p_hi = p.astype(BF16)
                p_lo = (p - p_hi.astype(F32)).astype(BF16)
                z = w * score
                part_sum = jnp.sum(z, axis=0, keepdims=True)
                if s:
                    part_sum = jnp.concatenate([jnp.zeros((1, s), F32), part_sum], axis=1)
                row_sum = row_sum + part_sum
                down[rows, :] += jnp.where(lanes == head, jnp.sum(z, axis=1, keepdims=True), 0.0)
                out = mm(p_hi, ogq[s:]) + mm(p_lo, ogq[s:])
                outs[n] = out if q == 0 else outs[n] + out
            across[pl.ds(head, 1), :] = row_sum
        for n, s in enumerate(starts):
            u_out[s : s + LANES, span] = outs[n]
        return 0

    lax.fori_loop(0, blocks, pair, 0)
    dcum_out[...] = across[...].T - down[...]
    wfull = jnp.where(causal, wsum[...], 0.0).astype(BF16)
    swapped = swapped.astype(BF16)
    dbc_out[...] = jnp.where(low_lanes, mm(wfull, swapped), mm(wfull, swapped, TN))


def close_kernel(
    side_ref, og_ref, x_ref, bc_ref, delta_ref, cum_ref, sig_ref, xdw_ref, dye_ref,
    u1_ref, u2_ref, dcum1_ref, dcum2_ref, dbc1_ref, dbc2_ref, turned_ref, alog_ref, skip_ref,
    mine_ref, other_ref,
    dx_out, dbc_out, ddt_out, small_out, *rest,
):
    sends, (pad, state) = rest[:-2], rest[-2:]
    count, inner = og_ref.shape
    heads = alog_ref.shape[1]
    blocks = inner // LANES
    half = inner // 2
    lanes = iota((1, LANES), 1)
    low_lanes = lanes < HALF
    first = side_ref[0] == 0
    pad[...] = jnp.zeros_like(pad)
    pad[0:1, :heads] = jnp.exp(alog_ref[...])
    pad[1:2, :heads] = skip_ref[...]
    rate, skip = pad[0:1, :], pad[1:2, :]
    state[:, :half] = jnp.where(first, mine_ref[...], other_ref[...])
    state[:, half:] = jnp.where(first, other_ref[...], mine_ref[...])
    delta, cum = delta_ref[...], cum_ref[...]
    total = cum[count - 1 : count, :]
    bc = bc_ref[...]
    bc_hi = bc.astype(BF16).astype(F32)
    bc_lo = bc - bc_hi
    zero = jnp.zeros_like(bc)

    def left_terms(hi, lo):
        first_half = jnp.where(low_lanes, hi, pltpu.roll(lo, HALF, 1))
        return jnp.concatenate([first_half, jnp.where(low_lanes, hi, zero)], axis=1).astype(BF16)

    b_left = left_terms(bc_hi, bc_lo)
    c_left = left_terms(pltpu.roll(bc_hi, HALF, 1), pltpu.roll(bc_lo, HALF, 1))
    fall2 = two_terms(jnp.exp(total - cum))
    delta2 = two_terms(delta)
    skip2 = three_terms(jnp.broadcast_to(skip, (8, LANES)))
    direct = jnp.zeros((count, LANES), F32)
    tails = jnp.zeros((count, LANES), F32)
    rises = jnp.zeros((count, LANES), F32)
    inner_sum = jnp.zeros((8, LANES), F32)
    skip_sum = jnp.zeros((8, LANES), F32)
    r1 = jnp.zeros((count, LANES), F32)
    r2 = jnp.zeros((count, LANES), F32)
    for j in range(blocks):
        span = slice(j * LANES, (j + 1) * LANES)
        st = state[:, span]
        stb = st.astype(BF16)
        st_lo = (st - stb.astype(F32)).astype(BF16)
        pad_rows = jnp.zeros((HALF, LANES), BF16)
        m_hi, s_hi, m_lo, s_lo = stb[:HALF], stb[HALF:], st_lo[:HALF], st_lo[HALF:]
        v1 = mm(b_left, jnp.concatenate([m_hi, m_hi, m_lo, pad_rows], axis=0))
        v2 = mm(c_left, jnp.concatenate([s_hi, s_hi, s_lo, pad_rows], axis=0))
        spread = spread_matrix(j, 2)
        gather = gather_matrix(j)
        gather2 = jnp.concatenate([gather, gather], axis=0)
        u_part = block(u1_ref, j) if j < blocks // 2 else block(u2_ref, j - blocks // 2)
        u = u_part + mm(fall2, spread) * v1
        og = og_ref[:, span].astype(F32)
        x = x_ref[:, span]
        skipx = mm(skip2, spread_matrix(j, 3))[0:1]
        dx_out[:, span] = (mm(delta2, spread) * u + skipx * og).astype(BF16)
        direct += mm(two_terms(x * u), gather2)
        xdw, dye = xdw_ref[:, span], dye_ref[:, span]
        tails += mm(two_terms(xdw.astype(F32) * v1), gather2)
        rises += mm(two_terms(dye.astype(F32) * v2), gather2)
        r1 += mm(xdw, stb, NT)
        r2 += mm(dye, stb, NT)
        gather32 = gather.astype(F32)
        prod = jnp.sum(st[:HALF] * st[HALF:], axis=0, keepdims=True)
        inner_sum += mm(jnp.broadcast_to(prod, (8, LANES)), gather32, precision=HIGH)
        prod = jnp.sum(x * og, axis=0, keepdims=True)
        skip_sum += mm(jnp.broadcast_to(prod, (8, LANES)), gather32, precision=HIGH)
    dbc_out[...] = (
        dbc1_ref[...] + dbc2_ref[...] + jnp.where(low_lanes, r1, r2)
    ).astype(BF16)
    later = (iota((count, count), 1) >= iota((count, count), 0)).astype(F32)
    before = (iota((count, count), 1) < iota((count, count), 0)).astype(F32)
    dg = (
        mm(later, dcum1_ref[...] + dcum2_ref[...] + rises, precision=HIGH)
        + mm(before, tails, precision=HIGH)
        + jnp.exp(total) * inner_sum[0:1]
    )
    dpre = jnp.where(lanes < heads, (direct - rate * dg) * sig_ref[...], 0.0)
    dpre_hi = dpre.astype(BF16).astype(F32)
    ddt_out[...] = (dpre_hi + pltpu.roll(dpre - dpre_hi, HALF, 1)).astype(BF16)
    sums = (
        jnp.sum(dg * (-rate) * delta, axis=0, keepdims=True),
        jnp.sum(dpre, axis=0, keepdims=True),
        jnp.where(lanes < heads, skip_sum[0:1], 0.0),
    )
    small = jnp.zeros((8, LANES), F32)
    for n, one in enumerate(sums):
        small = small + pltpu.roll(jnp.broadcast_to(one, (8, LANES)), 32 * (n + 1), 1)
    small_out[...] = small
    weight_part(turned_ref, dx_out, dbc_out, ddt_out, small_out, sends, True)


def weight_part(turned_ref, dx_ref, dbc_ref, ddt_ref, small_ref, outs, second):
    rows = turned_ref.shape[1] // 2
    part = slice(rows, 2 * rows) if second else slice(0, rows)
    at = 0
    blocks = dx_ref.shape[1] // LANES
    lanes = iota((1, LANES), 1)
    for n, out in enumerate(outs):
        turned = turned_ref[n, part, :]
        for k in range(out.shape[1] // LANES):
            span = slice(k * LANES, (k + 1) * LANES)
            if at < blocks:
                out[:, span] = mm(turned, block(dx_ref, at))
            elif at == blocks:
                out[:, span] = mm(turned, dbc_ref[...])
            else:
                both = mm(turned, ddt_ref[...])
                both = both + pltpu.roll(both, HALF, 1)
                out[:, span] = jnp.where(lanes < 32, both, small_ref[0:1, :])
            at += 1


def rest_kernel(
    turned_ref, dx_ref, dbc_ref, ddt_ref, small_ref, xw_ref, bcw_ref, dtw_ref, grad_out,
    *keeps_and_pad,
):
    keeps, pad = keeps_and_pad[:-1], keeps_and_pad[-1]
    weight_part(turned_ref, dx_ref, dbc_ref, ddt_ref, small_ref, keeps, False)
    heads = dtw_ref.shape[1]
    pad[...] = jnp.zeros_like(pad)
    pad[:, :heads] = dtw_ref[...].astype(F32)
    pad[:, HALF : HALF + heads] = dtw_ref[...].astype(F32)
    grad = mm(dx_ref[...], xw_ref[...], NT)
    grad += mm(dbc_ref[...], bcw_ref[...], NT)
    grad += mm(ddt_ref[...], pad[...].astype(BF16), NT)
    grad_out[...] = grad.astype(BF16)


VMEM = pl.BlockSpec(memory_space=pltpu.VMEM)
SMEM = pl.BlockSpec(memory_space=pltpu.SMEM)


def call(kernel, outs, scratch, args, cost, scalar=False, name=None, columns=None):
    specs = [SMEM if scalar and n == 0 else VMEM for n in range(len(args))]
    for n, spec in (columns or {}).items():
        specs[n] = spec
    return pl.pallas_call(
        kernel,
        name=name,
        grid=(1,) if columns else (),
        out_shape=[jax.ShapeDtypeStruct(shape, dtype) for shape, dtype in outs],
        in_specs=specs,
        out_specs=[VMEM] * len(outs),
        scratch_shapes=[pltpu.VMEM(shape, dtype) for shape, dtype in scratch],
        cost_estimate=pl.CostEstimate(
            flops=cost, bytes_accessed=cost // 256, transcendentals=0
        ),
        compiler_params=pltpu.CompilerParams(vmem_limit_bytes=40 * 1024 * 1024),
    )(*args)


def swap(value, axis, bit):
    return lax.ppermute(value, axis, [(k, k ^ bit) for k in range(lax.axis_size(axis))])


def slide(value, axis, step):
    count = lax.axis_size(axis)
    pairs = [(k, k + step) for k in range(count) if 0 <= k + step < count]
    return lax.ppermute(value, axis, pairs)


def bits_of(axis):
    return [(axis, 1 << n) for n in range(lax.axis_size(axis).bit_length() - 1)]


def scans(ahead, behind, logs, fillers):
    rows = ahead.shape[0]
    values, passed = [ahead, behind], [jnp.zeros_like(logs)] * 2
    totals, logs = [jnp.zeros_like(ahead)] * 2, [logs] * 2
    width, count = 1, lax.axis_size("seq") // 2
    results = []
    while width < count:
        last = 2 * width >= count
        sent = values
        if not last:
            sent = [jnp.concatenate([v, log], axis=0) for v, log in zip(values, logs)]
        gate = None
        if fillers:
            sent, gate = lax.optimization_barrier((sent, fillers[0][1]))
        got = [slide(v, "seq", 2 * width * d) for v, d in zip(sent, (1, -1))]
        if fillers:
            got, result = lax.optimization_barrier((got, fillers[0][0](gate)))
            results.append(result)
            fillers = fillers[1:]
        for n in range(2):
            new = got[n][:rows]
            totals[n] = totals[n] + jnp.exp(passed[n][0:1]) * new
            if not last:
                values[n] = values[n] + jnp.exp(logs[n][0:1]) * new
                passed[n] = passed[n] + got[n][rows:]
                logs[n] = logs[n] + got[n][rows:]
        width *= 2
    results.extend(run(gate) for run, gate in fillers)
    return totals[0], totals[1], results


def body(layer_in, out_grad, x_weight, bc_weight, dt_weight, a_log, dt_bias, skip_gain):
    inner = x_weight.shape[1]
    width = x_weight.shape[0]
    heads = dt_weight.shape[1]
    state = bc_weight.shape[1] // 2
    seq_in, og = layer_in[0], out_grad[0]
    count = seq_in.shape[0]
    tokens_all = count * lax.axis_size("seq") * layer_in.shape[0] * lax.axis_size("dp")
    inv_root = 1.0 / math.sqrt(tokens_all)
    devices = lax.axis_size(("seq", "dp"))
    rows = width // devices
    n_dp = lax.axis_size("dp")
    seq_at, dp_at = lax.axis_index("seq"), lax.axis_index("dp")
    me = seq_at * n_dp + dp_at
    side = (seq_at & 1).astype(jnp.int32)
    side1 = side.reshape(1)

    dp_bits, seq_bits = bits_of("dp"), bits_of("seq")
    start, dp_rest = dp_bits[:1], dp_bits[1:]
    orders = [
        start + dp_rest + seq_bits,
        start + seq_bits[:1] + dp_rest + seq_bits[1:],
        start + seq_bits[1:] + dp_rest + seq_bits[:1],
    ]
    offsets = np.zeros((8, width), np.int32)
    for n, order in enumerate(orders):
        for r in range(devices):
            mask = 0
            for k, (axis, bit) in enumerate(order):
                if (r >> (len(order) - 1 - k)) & 1:
                    mask ^= bit * (n_dp if axis == "seq" else 1)
            offsets[n, r * rows : (r + 1) * rows] = mask
    within = np.broadcast_to(np.arange(width, dtype=np.int32) % rows, (8, width))
    src = (me ^ jnp.asarray(offsets)) * rows + jnp.asarray(within)

    alog2, bias2, skip2 = (v.reshape(1, heads) for v in (a_log, dt_bias, skip_gain))
    head_shape = ((count, LANES), F32)
    wide_b = ((count, inner), BF16)
    half = inner // 2
    xf, bc, delta, cum, cumt, sig, xdw, dye, mine, send = call(
        first_kernel,
        [((count, inner), F32), head_shape, head_shape, head_shape, ((LANES, count), F32),
         head_shape, wide_b, wide_b] + [((2 * state + 8, half), F32)] * 2,
        [((count + 8, LANES), F32)],
        (side1, seq_in, og, x_weight, bc_weight, dt_weight, alog2, bias2),
        2_000_000_000, scalar=True, name="first",
    )

    got = swap(send, "seq", 1)
    (turned,) = call(
        turn_kernel, [((len(orders), width, count), BF16)], [], (seq_in, src),
        3_000_000_000, name="turn",
    )
    got, turned = lax.optimization_barrier((got, turned))

    def quad(part, og):
        column = pl.BlockSpec((count, half), lambda i: (0, part))
        return call(
            functools.partial(quad_kernel, part * half // LANES),
            [((count, half), F32), head_shape, head_shape],
            [((count, half), F32), ((count, half), F32), ((count, count), F32),
             ((LANES, count), F32), head_shape, ((count, count), F32)],
            (og, xf, bc, delta, cum, cumt),
            4_000_000_000, name="quad", columns={0: column, 1: column},
        )

    first = side == 0
    before, after = jnp.where(first, mine, got), jnp.where(first, got, mine)
    e0, l0, g0 = before[:state], before[state : 2 * state], before[2 * state :]
    e1, l1, g1 = after[:state], after[state : 2 * state], after[2 * state :]
    fillers = [(functools.partial(quad, 0), og), (functools.partial(quad, 1), og)]
    s_in, m_in, ((u1, dcum1, dbc1), (u2, dcum2, dbc2)) = scans(
        jnp.exp(g1[0:1]) * e0 + e1, l0 + jnp.exp(g0[0:1]) * l1, g0 + g1, fillers
    )
    s_second = jnp.exp(g0[0:1]) * s_in + e0
    m_first = jnp.exp(g1[0:1]) * m_in + l1
    both_first = jnp.concatenate([m_first, s_in], axis=0)
    both_second = jnp.concatenate([m_in, s_second], axis=0)
    other = swap(jnp.where(first, both_second, both_first), "seq", 1)
    mine = jnp.where(first, both_first, both_second)

    col_counts = [n * LANES for n in COLOR_BLOCKS]
    part_shapes = [((width // 2, n), F32) for n in col_counts]
    dx, dbc, ddt, small, *sends = call(
        close_kernel,
        [wide_b, ((count, LANES), BF16), ((count, LANES), BF16), ((8, LANES), F32)] + part_shapes,
        [((8, LANES), F32), ((2 * state, inner), F32)],
        (side1, og, xf, bc, delta, cum, sig, xdw, dye, u1, u2, dcum1, dcum2, dbc1, dbc2, turned,
         alog2, skip2, mine, other),
        2_000_000_000, scalar=True, name="close",
    )
    got = [swap(send, *order[0]) for send, order in zip(sends, orders)]
    grad, *keeps = call(
        rest_kernel,
        [((count, width), BF16)] + part_shapes,
        [((width, LANES), F32)],
        (turned, dx, dbc, ddt, small, x_weight, bc_weight, dt_weight),
        2_000_000_000, name="rest",
    )
    got, keeps = lax.optimization_barrier((got, keeps))
    for k in range(1, len(orders[0])):
        size = keeps[0].shape[0] // 2
        sends = [keep[size:] + new[size:] for keep, new in zip(keeps, got)]
        keeps, olds = [keep[:size] for keep in keeps], got
        got = [swap(send, *order[k]) for send, order in zip(sends, orders)]
        keeps = [keep + old[:size] for keep, old in zip(keeps, olds)]
        got, keeps = lax.optimization_barrier((got, keeps))
    final = jnp.concatenate([keep + new for keep, new in zip(keeps, got)], axis=1) * inv_root
    at = inner + 2 * state
    return (
        grad[None],
        final[:, :inner],
        final[:, inner:at],
        final[:, at : at + heads],
        final[0, at + 32 : at + 32 + heads],
        final[0, at + 64 : at + 64 + heads],
        final[0, at + 96 : at + 96 + heads],
    )


def solution(mesh):
    return jax.shard_map(
        body,
        mesh=mesh,
        in_specs=(P("dp", "seq", None), P("dp", "seq", None), P(), P(), P(), P(), P(), P()),
        out_specs=(
            P("dp", "seq", None),
            P(("seq", "dp"), None),
            P(("seq", "dp"), None),
            P(("seq", "dp"), None),
            P(),
            P(),
            P(),
        ),
        check_vma=False,
    )
```

```python
import functools
import math

import jax
import jax.numpy as jnp
import numpy as np
from jax import lax
from jax.experimental import pallas as pl
from jax.experimental.pallas import tpu as pltpu
from jax.sharding import PartitionSpec as P

LANES = 128
HALF = 64
HIGH = lax.Precision.HIGHEST
F32 = jnp.float32
BF16 = jnp.bfloat16
GROUPS = 1
ROUTES = ((9, 5),)
HOLDS = ((0,),)

NN = (((1,), (0,)), ((), ()))
NT = (((1,), (1,)), ((), ()))
TN = (((0,), (0,)), ((), ()))


def mm(a, b, dims=NN, precision=None):
    return lax.dot_general(a, b, dims, precision=precision, preferred_element_type=F32)


def iota(shape, axis):
    return lax.broadcasted_iota(jnp.int32, shape, axis)


def block(ref, j):
    return ref[:, j * LANES : (j + 1) * LANES]


def two_terms(f):
    hi = f.astype(BF16)
    lo = (f - hi.astype(F32)).astype(BF16)
    return jnp.concatenate([hi, lo], axis=1)


def three_terms(f):
    hi = f.astype(BF16)
    rest = f - hi.astype(F32)
    mid = rest.astype(BF16)
    lo = (rest - mid.astype(F32)).astype(BF16)
    return jnp.concatenate([hi, mid, lo], axis=1)


def spread_matrix(head, width, terms):
    row, lane = iota((LANES, width), 0), iota((LANES, width), 1)
    one = (row == head + lane // HALF).astype(F32).astype(BF16)
    return jnp.concatenate([one] * terms, axis=0)


def gather_matrix(head):
    row, lane = iota((LANES, LANES), 0), iota((LANES, LANES), 1)
    return (lane == head + row // HALF).astype(F32).astype(BF16)


def first_kernel(
    group, side_ref, in_hbm, og_hbm, xw_hbm, bcw_hbm, dtw_ref, alog_ref, bias_ref,
    x_out, xdw_out, dye_out, mine_out, send_out, bc_out, delta_out, cum_out, cumt_out, sig_out,
    pad, in_ref, bcw_ref, og_ref, xw_ref, sems,
):
    count, heads = in_ref.shape[0], dtw_ref.shape[0]
    width = og_ref.shape[2]
    half = og_hbm.shape[1] // 2
    copies = [
        pltpu.make_async_copy(in_hbm, in_ref, sems.at[0]),
        pltpu.make_async_copy(bcw_hbm, bcw_ref, sems.at[1]),
    ]
    for h in range(2):
        span = pl.ds(h * half + group * width, width)
        copies.append(pltpu.make_async_copy(xw_hbm.at[:, span], xw_ref.at[h], sems.at[2 + 2 * h]))
        copies.append(pltpu.make_async_copy(og_hbm.at[:, span], og_ref.at[h], sems.at[3 + 2 * h]))
    for copy in copies:
        copy.start()
    pad[...] = jnp.zeros_like(pad)
    pad[count : count + 1, :heads] = jnp.exp(alog_ref[...])
    pad[count + 1 : count + 2, :heads] = bias_ref[...]
    copies[0].wait()
    pad[:count, :heads] = mm(in_ref[...], dtw_ref[...], NT)
    rate = pad[count : count + 1, :]
    pre = pad[:count, :] + pad[count + 1 : count + 2, :]
    small = jnp.exp(-jnp.abs(pre))
    delta = jnp.maximum(pre, 0.0) + jnp.log1p(small)
    sig_out[...] = jnp.where(pre >= 0.0, 1.0, small) / (1.0 + small)
    decay = -rate * delta
    lower = (iota((count, count), 0) >= iota((count, count), 1)).astype(F32)
    cum = mm(lower, decay, precision=HIGH)
    total = cum[count - 1 : count, :]
    delta_out[...] = delta
    cum_out[...] = cum
    cumt_out[...] = cum.T
    copies[1].wait()
    bc = mm(in_ref[...], bcw_ref[...])
    bc_out[...] = bc
    turned = bc.T
    turned_hi = turned.astype(BF16).astype(F32)
    turned_lo = turned - turned_hi
    b_left = jnp.concatenate([turned_hi[:HALF], turned_lo[:HALF]], axis=0).astype(BF16)
    c_left = jnp.concatenate([turned_hi[HALF:], turned_lo[HALF:]], axis=0).astype(BF16)
    tail = two_terms(delta * jnp.exp(total - cum))
    rise = two_terms(jnp.exp(cum))
    sums = three_terms(jnp.broadcast_to(total, (8, LANES)))
    first = side_ref[0] == 0
    parts = []
    for h in range(2):
        span = slice(h * width, (h + 1) * width)
        spread3 = spread_matrix((h * half + group * width) // HALF, width, 3)
        spread2 = spread3[: 2 * LANES]
        copies[2 + 2 * h].wait()
        x = mm(in_ref[...], xw_ref[h])
        x_out[:, span] = x
        xdw = (x * mm(tail, spread2)).astype(BF16)
        xdw_out[:, span] = xdw
        copies[3 + 2 * h].wait()
        dye = (og_ref[h].astype(F32) * mm(rise, spread2)).astype(BF16)
        dye_out[:, span] = dye
        e_part, l_part = mm(b_left, xdw), mm(c_left, dye)
        parts.append((
            e_part[:HALF] + e_part[HALF:], l_part[:HALF] + l_part[HALF:], mm(sums, spread3)
        ))
    for n, (low, high) in enumerate(zip(*parts)):
        rows = slice(n * HALF, n * HALF + low.shape[0])
        mine_out[rows, :] = jnp.where(first, low, high)
        send_out[rows, :] = jnp.where(first, high, low)


def turn_kernel(in_ref, src_ref, turned_out):
    width = in_ref.shape[1]
    for n in range(turned_out.shape[0]):
        chosen = (iota((width, width), 0) == src_ref[n : n + 1, :]).astype(F32).astype(BF16)
        turned_out[n] = mm(in_ref[...], chosen).T.astype(BF16)


def block_at(group, blocks, half_blocks, j):
    skip = half_blocks - blocks
    if isinstance(j, int):
        return group * blocks + j + (skip if j >= blocks else 0)
    return group * blocks + j + jnp.where(j >= blocks, skip, 0)


def quad_kernel(
    group, og_ref, x_ref, bc_ref, delta_ref, cum_ref, cumt_ref,
    u_out, dcum_out, dbc_out, cumx, deltax, wsum, across, down, scores,
):
    count, part = x_ref.shape
    blocks = part // LANES
    place = functools.partial(block_at, group, blocks // 2, og_ref.shape[1] // LANES // 2)
    lanes = iota((1, LANES), 1)
    low_lanes = lanes < HALF
    cum3, delta2 = three_terms(cum_ref[...]), two_terms(delta_ref[...])
    for j in range(blocks):
        spread3 = spread_matrix(2 * place(j), LANES, 3)
        cumx[:, j * LANES : (j + 1) * LANES] = mm(cum3, spread3)
        deltax[:, j * LANES : (j + 1) * LANES] = mm(delta2, spread3[: 2 * LANES])
    bc = bc_ref[...]
    swapped = pltpu.roll(bc, HALF, 1)
    causal = iota((count, count), 1) >= iota((count, count), 0)
    scores[...] = jnp.where(causal, mm(jnp.where(low_lanes, bc, 0.0), swapped, NT, HIGH), 0.0)
    wsum[...] = jnp.zeros_like(wsum)
    across[...] = jnp.zeros_like(across)
    down[...] = jnp.zeros_like(down)
    starts = list(range(0, count, LANES))

    def pair(j, _):
        span = pl.ds(pl.multiple_of(j * LANES, LANES), LANES)
        at = place(j)
        og = og_ref[:, pl.ds(pl.multiple_of(at * LANES, LANES), LANES)].astype(F32)
        og_turned = pltpu.roll(og, HALF, 1)
        x = x_ref[:, span] * deltax[:, span]
        x_hi = x.astype(BF16).astype(F32)
        x_lo = pltpu.roll(x - x_hi, HALF, 1)
        cumj = cumx[:, span]
        outs = [None] * len(starts)
        for q in range(2):
            mine = low_lanes if q == 0 else jnp.logical_not(low_lanes)
            head = 2 * at + q
            xq = jnp.where(mine, x_hi, x_lo).astype(BF16)
            og_both = jnp.where(mine, og, og_turned).astype(BF16)
            ogq = jnp.where(mine, og, 0.0).astype(BF16)
            row = cumt_ref[pl.ds(head, 1), :]
            row_sum = jnp.zeros((1, count), F32)
            for n, s in enumerate(starts):
                rows = slice(s, s + LANES)
                d = mm(xq[rows], og_both[s:], NT)
                col = cumj[rows, q * HALF : q * HALF + 1]
                a = jnp.exp(jnp.minimum(row[:, s:] - col, 0.0))
                score = scores[rows, s:]
                w = a * d
                wsum[rows, s:] += w
                p = a * score
                p_hi = p.astype(BF16)
                p_lo = (p - p_hi.astype(F32)).astype(BF16)
                z = w * score
                part_sum = jnp.sum(z, axis=0, keepdims=True)
                if s:
                    part_sum = jnp.concatenate([jnp.zeros((1, s), F32), part_sum], axis=1)
                row_sum = row_sum + part_sum
                down[rows, :] += jnp.where(lanes == head, jnp.sum(z, axis=1, keepdims=True), 0.0)
                out = mm(p_hi, ogq[s:]) + mm(p_lo, ogq[s:])
                outs[n] = out if q == 0 else outs[n] + out
            across[pl.ds(head, 1), :] = row_sum
        for n, s in enumerate(starts):
            u_out[s : s + LANES, span] = outs[n]
        return 0

    lax.fori_loop(0, blocks, pair, 0)
    dcum_out[...] = across[...].T - down[...]
    wfull = jnp.where(causal, wsum[...], 0.0).astype(BF16)
    swapped = swapped.astype(BF16)
    dbc_out[...] = jnp.where(low_lanes, mm(wfull, swapped), mm(wfull, swapped, TN))


def close_kernel(group, last, *refs):
    (side_ref, og_ref, x_ref, bc_ref, delta_ref, cum_ref, xdw_ref, dye_ref, u_ref, turned_ref,
     skip_ref, mine_ref, other_ref, dcum_ref, dbcq_ref) = refs[:15]
    refs = list(refs[15:])
    prev_ref = refs.pop(0) if group else None
    if last:
        sig_ref, alog_ref = refs.pop(0), refs.pop(0)
        dx_out, send_out, dbc_out, ddt_out, small_out, pad = refs
    else:
        dx_out, send_out, acc_out, pad = refs
    count, inner = og_ref.shape
    heads = skip_ref.shape[1]
    blocks = x_ref.shape[1] // LANES
    place = functools.partial(block_at, group, blocks // 2, inner // LANES // 2)
    lanes = iota((1, LANES), 1)
    low_lanes = lanes < HALF
    first = side_ref[0] == 0
    pad[...] = jnp.zeros_like(pad)
    pad[1:2, :heads] = skip_ref[...]
    skip = pad[1:2, :]
    delta, cum = delta_ref[...], cum_ref[...]
    total = cum[count - 1 : count, :]
    bc = bc_ref[...]
    bc_hi = bc.astype(BF16).astype(F32)
    bc_lo = bc - bc_hi
    zero = jnp.zeros_like(bc)

    def left_terms(hi, lo):
        first_half = jnp.where(low_lanes, hi, pltpu.roll(lo, HALF, 1))
        return jnp.concatenate([first_half, jnp.where(low_lanes, hi, zero)], axis=1).astype(BF16)

    b_left = left_terms(bc_hi, bc_lo)
    c_left = left_terms(pltpu.roll(bc_hi, HALF, 1), pltpu.roll(bc_lo, HALF, 1))
    fall2 = two_terms(jnp.exp(total - cum))
    delta2 = two_terms(delta)
    skip2 = three_terms(jnp.broadcast_to(skip, (8, LANES)))
    if prev_ref is None:
        direct, tails, rises, r1, r2 = [jnp.zeros((count, LANES), F32)] * 5
        inner_sum, skip_sum = [jnp.zeros((8, LANES), F32)] * 2
        dcum, dbcq = dcum_ref[...], dbcq_ref[...]
    else:
        direct, tails, rises, r1, r2, dcum, dbcq = (
            prev_ref[n * count : (n + 1) * count, :] for n in range(7)
        )
        inner_sum, skip_sum = prev_ref[7 * count : 7 * count + 8, :], prev_ref[7 * count + 8 :, :]
        dcum, dbcq = dcum + dcum_ref[...], dbcq + dbcq_ref[...]
    for j in range(blocks):
        span = slice(j * LANES, (j + 1) * LANES)
        near = slice(j % (blocks // 2) * LANES, (j % (blocks // 2) + 1) * LANES)
        mine, other = mine_ref[:, near], other_ref[:, near]
        st = jnp.where(first, mine, other) if j < blocks // 2 else jnp.where(first, other, mine)
        stb = st.astype(BF16)
        st_lo = (st - stb.astype(F32)).astype(BF16)
        pad_rows = jnp.zeros((HALF, LANES), BF16)
        m_hi, s_hi, m_lo, s_lo = stb[:HALF], stb[HALF:], st_lo[:HALF], st_lo[HALF:]
        v1 = mm(b_left, jnp.concatenate([m_hi, m_hi, m_lo, pad_rows], axis=0))
        v2 = mm(c_left, jnp.concatenate([s_hi, s_hi, s_lo, pad_rows], axis=0))
        head = 2 * place(j)
        spread3 = spread_matrix(head, LANES, 3)
        spread = spread3[: 2 * LANES]
        gather = gather_matrix(head)
        gather2 = jnp.concatenate([gather, gather], axis=0)
        u = u_ref[:, span] + mm(fall2, spread) * v1
        og = block(og_ref, place(j)).astype(F32)
        x = x_ref[:, span]
        skipx = mm(skip2, spread3)[0:1]
        dx_out[:, span] = (mm(delta2, spread) * u + skipx * og).astype(BF16)
        direct += mm(two_terms(x * u), gather2)
        xdw, dye = xdw_ref[:, span], dye_ref[:, span]
        tails += mm(two_terms(xdw.astype(F32) * v1), gather2)
        rises += mm(two_terms(dye.astype(F32) * v2), gather2)
        r1 += mm(xdw, stb, NT)
        r2 += mm(dye, stb, NT)
        gather32 = gather.astype(F32)
        prod = jnp.sum(st[:HALF] * st[HALF:], axis=0, keepdims=True)
        inner_sum += mm(jnp.broadcast_to(prod, (8, LANES)), gather32, precision=HIGH)
        prod = jnp.sum(x * og, axis=0, keepdims=True)
        skip_sum += mm(jnp.broadcast_to(prod, (8, LANES)), gather32, precision=HIGH)
    if not last:
        for n, value in enumerate((direct, tails, rises, r1, r2, dcum, dbcq)):
            acc_out[n * count : (n + 1) * count, :] = value
        acc_out[7 * count : 7 * count + 8, :] = inner_sum
        acc_out[7 * count + 8 :, :] = skip_sum
        weight_part(turned_ref, dx_out, None, send_out, group, True)
        return
    pad[0:1, :heads] = jnp.exp(alog_ref[...])
    rate = pad[0:1, :]
    dbc_out[...] = (dbcq + jnp.where(low_lanes, r1, r2)).astype(BF16)
    later = (iota((count, count), 1) >= iota((count, count), 0)).astype(F32)
    before = (iota((count, count), 1) < iota((count, count), 0)).astype(F32)
    dg = (
        mm(later, dcum + rises, precision=HIGH)
        + mm(before, tails, precision=HIGH)
        + jnp.exp(total) * inner_sum[0:1]
    )
    dpre = jnp.where(lanes < heads, (direct - rate * dg) * sig_ref[...], 0.0)
    dpre_hi = dpre.astype(BF16).astype(F32)
    ddt_out[...] = (dpre_hi + pltpu.roll(dpre - dpre_hi, HALF, 1)).astype(BF16)
    sums = (
        jnp.sum(dg * (-rate) * delta, axis=0, keepdims=True),
        jnp.sum(dpre, axis=0, keepdims=True),
        jnp.where(lanes < heads, skip_sum[0:1], 0.0),
    )
    small = jnp.zeros((8, LANES), F32)
    for n, one in enumerate(sums):
        small = small + pltpu.roll(jnp.broadcast_to(one, (8, LANES)), 32 * (n + 1), 1)
    small_out[...] = small
    weight_part(turned_ref, dx_out, (dbc_out, ddt_out, small_out), send_out, group, True)


def weight_part(turned_ref, dx_ref, more, out, group, second):
    rows = turned_ref.shape[1] // 2
    part = slice(rows, 2 * rows) if second else slice(0, rows)
    blocks = dx_ref.shape[1] // LANES
    lanes = iota((1, LANES), 1)
    at = 0
    for n, size in enumerate(ROUTES[group]):
        if not size:
            continue
        turned = turned_ref[n, part, :]
        wide = min(at + size, blocks) - at
        if wide > 0:
            span = slice(at * LANES, (at + wide) * LANES)
            out[:, span] = mm(turned, dx_ref[:, span])
        for k in range(max(at, blocks), at + size):
            span = slice(k * LANES, (k + 1) * LANES)
            if k == blocks:
                out[:, span] = mm(turned, more[0][...])
            else:
                both = mm(turned, more[1][...])
                both = both + pltpu.roll(both, HALF, 1)
                out[:, span] = jnp.where(lanes < 32, both, more[2][0:1, :])
        at += size


def keep_kernel(group, turned_ref, dx_ref, *rest):
    weight_part(turned_ref, dx_ref, rest[:-1], rest[-1], group, False)


def grad_kernel(dbc_ref, ddt_ref, xw_ref, bcw_ref, dtw_ref, *rest):
    dx_refs, (grad_out, pad) = rest[:-2], rest[-2:]
    heads = dtw_ref.shape[0]
    half = xw_ref.shape[1] // 2
    pad[...] = jnp.zeros_like(pad)
    pad[:heads, :] = dtw_ref[...].astype(F32)
    pad[HALF : HALF + heads, :] = dtw_ref[...].astype(F32)
    grad = mm(dbc_ref[...], bcw_ref[...], NT)
    grad += mm(ddt_ref[...], pad[...].astype(BF16))
    for group, dx_ref in enumerate(dx_refs):
        width = dx_ref.shape[1] // 2
        for h in range(2):
            span = slice(h * half + group * width, h * half + (group + 1) * width)
            grad += mm(dx_ref[:, h * width : (h + 1) * width], xw_ref[:, span], NT)
    grad_out[...] = grad.astype(BF16)


VMEM = pl.BlockSpec(memory_space=pltpu.VMEM)
SMEM = pl.BlockSpec(memory_space=pltpu.SMEM)


HBM = pl.BlockSpec(memory_space=pltpu.HBM)


def call(kernel, outs, scratch, args, flops, name, specs=None, limit=40):
    return pl.pallas_call(
        kernel,
        name=name,
        out_shape=[jax.ShapeDtypeStruct(shape, dtype) for shape, dtype in outs],
        in_specs=[(specs or {}).get(n, VMEM) for n in range(len(args))],
        out_specs=[VMEM] * len(outs),
        scratch_shapes=[
            pltpu.VMEM(*one) if isinstance(one, tuple) else one for one in scratch
        ],
        cost_estimate=pl.CostEstimate(
            flops=flops, bytes_accessed=flops // 256, transcendentals=0
        ),
        compiler_params=pltpu.CompilerParams(vmem_limit_bytes=limit * 1024 * 1024),
    )(*args)


def swap(value, axis, bit):
    return lax.ppermute(value, axis, [(k, k ^ bit) for k in range(lax.axis_size(axis))])


def slide(value, axis, step):
    count = lax.axis_size(axis)
    pairs = [(k, k + step) for k in range(count) if 0 <= k + step < count]
    return lax.ppermute(value, axis, pairs)


def swap_by_parity(value, both, k):
    n_dp = lax.axis_size("dp")
    flips = [bit * (n_dp if axis == "seq" else 1) for axis, bit in (order[k] for order in both)]
    pairs = [(n, n ^ flips[n % n_dp % 2]) for n in range(lax.axis_size("seq") * n_dp)]
    return lax.ppermute(value, ("seq", "dp"), pairs)


def bits_of(axis):
    return [(axis, 1 << n) for n in range(lax.axis_size(axis).bit_length() - 1)]


def scans(ahead, behind, logs):
    rows = ahead.shape[0]
    values, passed = [ahead, behind], [jnp.zeros_like(logs)] * 2
    totals, logs = [jnp.zeros_like(ahead)] * 2, [logs] * 2
    width, count = 1, lax.axis_size("seq") // 2
    while width < count:
        last = 2 * width >= count
        sent = values
        if not last:
            sent = [jnp.concatenate([v, log], axis=0) for v, log in zip(values, logs)]
        got, _ = yield (
            [functools.partial(slide, v, "seq", 2 * width * d) for v, d in zip(sent, (1, -1))],
            None,
            0,
        )
        for n in range(2):
            new = got[n][:rows]
            totals[n] = totals[n] + jnp.exp(passed[n][0:1]) * new
            if not last:
                values[n] = values[n] + jnp.exp(logs[n][0:1]) * new
                passed[n] = passed[n] + got[n][rows:]
                logs[n] = logs[n] + got[n][rows:]
        width *= 2
    return totals


def halves_of(where_ref, mine_ref, got_ref):
    first = where_ref[0] == 0
    mine, got = mine_ref[...], got_ref[...]
    return jnp.where(first, mine, got), jnp.where(first, got, mine)


def pair_kernel(where_ref, mine_ref, got_ref, send_out, ahead_out, behind_out, decay_out):
    state = send_out.shape[0]
    before, after = halves_of(where_ref, mine_ref, got_ref)
    g0, g1 = jnp.exp(before[2 * state :]), jnp.exp(after[2 * state :])
    ahead = g1[0:1] * before[:state] + after[:state]
    behind = before[state : 2 * state] + g0[0:1] * after[state : 2 * state]
    send_out[...] = jnp.where(where_ref[1] == 0, ahead, behind)
    ahead_out[...], behind_out[...], decay_out[...] = ahead, behind, g0 * g1


def pass_kernel(turn, where_ref, ahead_ref, behind_ref, decay_ref, got_ref, send_out):
    straight = where_ref[1] == (1 if turn == 0 else 2)
    own = jnp.where(straight, ahead_ref[...], behind_ref[...])
    send_out[...] = own + decay_ref[0:1, :] * got_ref[...]


def spread_kernel(where_ref, mine_ref, got_ref, got1_ref, got2_ref, got3_ref, mine_out, send_out):
    state = got1_ref.shape[0]
    pair = where_ref[1]
    got1, got2, got3 = got1_ref[...], got2_ref[...], got3_ref[...]
    zero = jnp.zeros_like(got1)
    middle, low = jnp.where(pair == 1, got1, got2), jnp.where(pair == 1, got2, got1)
    inside = jnp.logical_and(pair > 0, pair < 3)
    s_in = jnp.where(inside, middle, jnp.where(pair == 3, got3, zero))
    m_in = jnp.where(inside, low, jnp.where(pair == 0, got3, zero))
    before, after = halves_of(where_ref, mine_ref, got_ref)
    s_second = jnp.exp(before[2 * state : 2 * state + 1]) * s_in + before[:state]
    m_first = jnp.exp(after[2 * state : 2 * state + 1]) * m_in + after[state : 2 * state]
    first = where_ref[0] == 0
    mine_out[:state] = jnp.where(first, m_first, m_in)
    mine_out[state:] = jnp.where(first, s_in, s_second)
    send_out[:state] = jnp.where(first, m_in, m_first)
    send_out[state:] = jnp.where(first, s_second, s_in)


def exchange_of_four(mine, send, where, state):
    one = ((state, mine.shape[1]), F32)
    two = ((2 * state, mine.shape[1]), F32)
    (got,), _ = yield [functools.partial(swap, send, "seq", 1)], None, 0
    send, ahead, behind, decay = call(
        pair_kernel, [one, one, one, ((8, mine.shape[1]), F32)], [], (where, mine, got),
        1_000_000, "pair", {0: SMEM},
    )

    def hop(value, pairs):
        return [functools.partial(hop_pairs, value, pairs)], None, 0

    (got1,), _ = yield hop(send, ((0, 1), (3, 2)))
    gots = [got1]
    for turn, pairs in enumerate((((1, 2), (2, 1)), ((1, 0), (2, 3)))):
        (send,) = call(
            functools.partial(pass_kernel, turn), [one], [],
            (where, ahead, behind, decay, gots[-1]), 1_000_000, f"pass{turn}", {0: SMEM},
        )
        (new,), _ = yield hop(send, pairs)
        gots.append(new)
    mine, send = call(
        spread_kernel, [two, two], [], (where, mine, got, *gots), 1_000_000, "spread", {0: SMEM},
    )
    (other,), mine = yield [functools.partial(swap, send, "seq", 1)], mine, 0
    return mine, other


def hop_pairs(value, pairs):
    return lax.ppermute(
        value, "seq", [(2 * one + k, 2 * to + k) for one, to in pairs for k in range(2)]
    )


def exchange(mine, send, first, state):
    (got,), _ = yield [functools.partial(swap, send, "seq", 1)], None, 0
    before, after = jnp.where(first, mine, got), jnp.where(first, got, mine)
    e0, l0, g0 = before[:state], before[state : 2 * state], before[2 * state :]
    e1, l1, g1 = after[:state], after[state : 2 * state], after[2 * state :]
    s_in, m_in = yield from scans(
        jnp.exp(g1[0:1]) * e0 + e1, l0 + jnp.exp(g0[0:1]) * l1, g0 + g1
    )
    s_second = jnp.exp(g0[0:1]) * s_in + e0
    m_first = jnp.exp(g1[0:1]) * m_in + l1
    both_first = jnp.concatenate([m_first, s_in], axis=0)
    both_second = jnp.concatenate([m_in, s_second], axis=0)
    send = jnp.where(first, both_second, both_first)
    mine = jnp.where(first, both_first, both_second)
    (other,), mine = yield [functools.partial(swap, send, "seq", 1)], mine, 0
    return mine, other


def scatter(send, make_keep, sizes, orders, holds):
    orders = [order for size, order in zip(sizes, orders) if size]
    sizes = [size for size in sizes if size]
    (got,), keep = yield [functools.partial(swap_by_parity, send, orders[0], 0)], make_keep(), holds[0]
    spans, at = [], 0
    for size in sizes:
        spans.append(slice(at * LANES, (at + size) * LANES))
        at += size
    keeps, gots = [keep[:, span] for span in spans], [got[:, span] for span in spans]
    for k in range(1, len(orders[0][0])):
        size = keeps[0].shape[0] // 2
        sends = [one[size:] + new[size:] for one, new in zip(keeps, gots)]
        keeps = [one[:size] + new[:size] for one, new in zip(keeps, gots)]
        gots, keeps = yield (
            [functools.partial(swap_by_parity, one, both, k) for one, both in zip(sends, orders)],
            keeps,
            holds[k] if k < len(holds) else 0,
        )
    return list(zip(keeps, gots))


def drive(programs, starts, filled, fillers, token):
    results = [None] * len(programs)
    ready, flying = {}, {}
    phase, pending = 0, list(range(len(programs)))
    while pending or ready or flying:
        for n in [n for n in pending if phase >= starts[n]]:
            pending.remove(n)
            ready[n] = None
        for n in list(ready):
            try:
                runs, more, hold = programs[n].send(ready.pop(n))
                flying[n] = (runs, more, phase + hold)
            except StopIteration as stop:
                results[n] = stop.value
        for n, (runs, more, due) in list(flying.items()):
            flying[n] = ([run() if callable(run) else run for run in runs], more, due)
        extra = {key: run(token) for key, run in fillers.get(phase, ())}
        sent = {n: (runs, more) for n, (runs, more, due) in flying.items() if due <= phase}
        if sent or extra:
            sent, extra, token = lax.optimization_barrier((sent, extra, token))
        for n in sent:
            del flying[n]
        filled.update(extra)
        ready.update(sent)
        phase += 1
    for later in sorted(fillers):
        if later >= phase:
            filled.update({key: run(token) for key, run in fillers[later]})
    return results


def body(layer_in, out_grad, x_weight, bc_weight, dt_weight, a_log, dt_bias, skip_gain):
    inner = x_weight.shape[1]
    width = x_weight.shape[0]
    heads = dt_weight.shape[1]
    state = bc_weight.shape[1] // 2
    seq_in, og = layer_in[0], out_grad[0]
    count = seq_in.shape[0]
    tokens_all = count * lax.axis_size("seq") * layer_in.shape[0] * lax.axis_size("dp")
    inv_root = 1.0 / math.sqrt(tokens_all)
    devices = lax.axis_size(("seq", "dp"))
    rows = width // devices
    n_dp = lax.axis_size("dp")
    seq_at, dp_at = lax.axis_index("seq"), lax.axis_index("dp")
    me = seq_at * n_dp + dp_at
    side = (seq_at & 1).astype(jnp.int32)
    side1 = side.reshape(1)
    where = jnp.stack([seq_at & 1, seq_at >> 1]).astype(jnp.int32)

    dp_bits, seq_bits = bits_of("dp"), bits_of("seq")
    start, dp_rest = dp_bits[:1], dp_bits[1:]
    y_bit, z_bits = seq_bits[:1], seq_bits[1:]
    orders = [
        (start + dp_rest + y_bit + z_bits, start + y_bit + dp_rest + z_bits[::-1]),
        (
            start + z_bits[:1] + dp_rest + y_bit + z_bits[1:],
            start + z_bits[:1] + y_bit + dp_rest + z_bits[1:],
        ),
    ]
    offsets = np.zeros((2, 8, width), np.int32)
    for n, both in enumerate(orders):
        for parity in range(2):
            for r in range(devices):
                mask = 0
                order = both[parity ^ (r >> (len(both[0]) - 1))]
                for k, (axis, bit) in enumerate(order):
                    if (r >> (len(order) - 1 - k)) & 1:
                        mask ^= bit * (n_dp if axis == "seq" else 1)
                offsets[parity, n, r * rows : (r + 1) * rows] = mask
    offsets = jnp.where((dp_at & 1) == 0, jnp.asarray(offsets[0]), jnp.asarray(offsets[1]))
    within = np.broadcast_to(np.arange(width, dtype=np.int32) % rows, (8, width))
    src = (me ^ offsets) * rows + jnp.asarray(within)

    alog2, bias2, skip2 = (v.reshape(1, heads) for v in (a_log, dt_bias, skip_gain))
    dtw = dt_weight.T
    head_shape = ((count, LANES), F32)
    part = inner // GROUPS
    half = part // 2
    part_b = ((count, part), BF16)
    first = side == 0
    filled = {}

    def run_first(group, og):
        return call(
            functools.partial(first_kernel, group),
            [((count, part), F32), part_b, part_b] + [((2 * state + 8, half), F32)] * 2
            + [head_shape] * 3 + [((LANES, count), F32), head_shape],
            [((count + 8, LANES), F32), (seq_in.shape, BF16), (bc_weight.shape, BF16),
             ((2, count, half), BF16), ((2, width, half), BF16), pltpu.SemaphoreType.DMA((6,))],
            (side1, seq_in, og, x_weight, bc_weight, dtw, alog2, bias2),
            1_000_000_000, f"first{group}", {0: SMEM, 1: HBM, 2: HBM, 3: HBM, 4: HBM},
            60,
        )

    def run_turn(_):
        return call(
            turn_kernel, [((len(orders), width, count), BF16)], [], (seq_in, src),
            3_000_000_000, "turn",
        )[0]

    filled["first", 0] = run_first(0, og)
    bc, delta, cum, cumt, sig = filled["first", 0][5:]

    def run_quad(group, og):
        return call(
            functools.partial(quad_kernel, group),
            [((count, part), F32), head_shape, head_shape],
            [((count, part), F32), ((count, part), F32), ((count, count), F32),
             ((LANES, count), F32), head_shape, ((count, count), F32)],
            (og, filled["first", group][0], bc, delta, cum, cumt),
            4_000_000_000, f"quad{group}", None, 60,
        )

    dxs, mores, accs = {}, {}, {}

    def program(group):
        last = group == GROUPS - 1
        xf, xdw, dye, mine, send = filled["first", group][:5]
        if len(seq_bits) == 3:
            mine, other = yield from exchange_of_four(mine, send, where, state)
        else:
            mine, other = yield from exchange(mine, send, first, state)
        u, dcum, dbcq = filled["quad", group]
        turned = filled["turn"]
        columns = sum(ROUTES[group]) * LANES
        args = [side1, og, xf, bc, delta, cum, xdw, dye, u, turned, skip2, mine, other, dcum, dbcq]
        outs = [part_b, ((width // 2, columns), F32)]
        if group:
            args.append(accs[group - 1])
        if last:
            args += [sig, alog2]
            outs += [((count, LANES), BF16)] * 2 + [((8, LANES), F32)]
        else:
            outs += [((7 * count + 16, LANES), F32)]
        dx, out_send, *more = call(
            functools.partial(close_kernel, group, last), outs, [((8, LANES), F32)], args,
            1_000_000_000, f"close{group}", {0: SMEM},
        )
        dxs[group] = dx
        if last:
            mores["last"] = more
        else:
            accs[group] = more[0]
            more = []

        def keep():
            return call(
                functools.partial(keep_kernel, group), [((width // 2, columns), F32)], [],
                [turned, dx, *more], 500_000_000, f"keep{group}",
            )[0]

        return (yield from scatter(out_send, keep, ROUTES[group], orders, HOLDS[group]))

    def run_grad(_):
        dbc, ddt, _ = mores["last"]
        return call(
            grad_kernel, [((count, width), BF16)], [((LANES, width), F32)],
            [dbc, ddt, x_weight, bc_weight, dtw] + [dxs[n] for n in range(GROUPS)],
            1_000_000_000, "grad",
        )[0]

    steps = len(dp_bits) + len(seq_bits)
    ahead = 5 if len(seq_bits) == 3 else 1 + len(seq_bits)
    fillers = {n: [] for n in range(64)}
    for group in range(GROUPS):
        if group:
            fillers[group - 1].append((("first", group), functools.partial(run_first, group)))
        fillers[group].append((("quad", group), functools.partial(run_quad, group)))
    fillers[2].append(("turn", run_turn))
    fillers[GROUPS - 1 + ahead + 1].append(("grad", run_grad))
    results = drive(
        [program(n) for n in range(GROUPS)], list(range(GROUPS)), filled, fillers, og
    )
    blocks = inner // LANES
    pieces = {}
    for group in range(GROUPS):
        place = functools.partial(block_at, group, part // LANES // 2, blocks // 2)
        at = 0
        for size, pair in zip([size for size in ROUTES[group] if size], results[group]):
            for k in range(size):
                j = at + k
                to = place(j) if j < part // LANES else blocks + j - part // LANES
                pieces[to] = (pair, slice(k * LANES, (k + 1) * LANES))
            at += size

    def total(n):
        (one, new), span = pieces[n]
        return (one[:, span] + new[:, span]) * inv_root

    ends = total(blocks + 1)
    return (
        filled["grad"][None],
        jnp.concatenate([total(n) for n in range(blocks)], axis=1),
        total(blocks),
        ends[:, :heads],
        ends[0, 32 : 32 + heads],
        ends[0, 64 : 64 + heads],
        ends[0, 96 : 96 + heads],
    )


def solution(mesh):
    return jax.shard_map(
        body,
        mesh=mesh,
        in_specs=(P("dp", "seq", None), P("dp", "seq", None), P(), P(), P(), P(), P(), P()),
        out_specs=(
            P("dp", "seq", None),
            P(("seq", "dp"), None),
            P(("seq", "dp"), None),
            P(("seq", "dp"), None),
            P(),
            P(),
            P(),
        ),
        check_vma=False,
    )
```

```python
import functools
import math

import jax
import jax.numpy as jnp
import numpy as np
from jax import lax
from jax.experimental import pallas as pl
from jax.experimental.pallas import tpu as pltpu
from jax.sharding import PartitionSpec as P

LANES = 128
HALF = 64
HIGH = lax.Precision.HIGHEST
F32 = jnp.float32
BF16 = jnp.bfloat16
ROUTES = (9, 5)
PARTS = 3
HOLDS = ({0: 1}, {1: 1})
GRAD_AT = 2

NN = (((1,), (0,)), ((), ()))
NT = (((1,), (1,)), ((), ()))
TN = (((0,), (0,)), ((), ()))


def mm(a, b, dims=NN, precision=None):
    return lax.dot_general(a, b, dims, precision=precision, preferred_element_type=F32)


def iota(shape, axis):
    return lax.broadcasted_iota(jnp.int32, shape, axis)


def block(ref, j):
    return ref[:, j * LANES : (j + 1) * LANES]


def two_terms(f):
    hi = f.astype(BF16)
    lo = (f - hi.astype(F32)).astype(BF16)
    return jnp.concatenate([hi, lo], axis=1)


def three_terms(f):
    hi = f.astype(BF16)
    rest = f - hi.astype(F32)
    mid = rest.astype(BF16)
    lo = (rest - mid.astype(F32)).astype(BF16)
    return jnp.concatenate([hi, mid, lo], axis=1)


def spread_matrix(head, width, terms):
    row, lane = iota((LANES, width), 0), iota((LANES, width), 1)
    one = (row == head + lane // HALF).astype(F32).astype(BF16)
    return jnp.concatenate([one] * terms, axis=0)


def gather_matrix(head):
    row, lane = iota((LANES, LANES), 0), iota((LANES, LANES), 1)
    return (lane == head + row // HALF).astype(F32).astype(BF16)


def add_terms(product):
    return sum(product[:, n * LANES : (n + 1) * LANES] for n in range(product.shape[1] // LANES))


def sum_rows(matrix, f):
    return add_terms(mm(matrix.astype(F32).astype(BF16), three_terms(f)))


def head_sums(rows, start):
    row, lane = iota((LANES, LANES), 0), iota((LANES, LANES), 1)
    one = (row // HALF == lane % 2).astype(F32).astype(BF16)
    each = mm(three_terms(rows), jnp.concatenate([one] * 3, axis=0))
    row, lane = iota(rows.shape, 0), iota(rows.shape, 1)
    return jnp.sum(jnp.where(lane // 2 == row + start // 2, each, 0.0), axis=0, keepdims=True)


def first_kernel(
    in_hbm, og_hbm, xw_hbm, bcw_hbm, dtw_ref, alog_ref, bias_ref,
    mine_out, send1_out, send2_out, bc_out, delta_out, cum_out, cumt_out, sig_out,
    x_hbm, xdw_hbm, dye_hbm,
    pad, in_ref, bcw_ref, og_ref, xw_ref, x_ref, xdw_ref, dye_ref, sems, out_sems,
):
    count, heads = in_ref.shape[0], dtw_ref.shape[0]
    inner = og_ref.shape[1]
    copies = [
        pltpu.make_async_copy(far, near, sems.at[n])
        for n, (far, near) in enumerate(
            ((in_hbm, in_ref), (bcw_hbm, bcw_ref), (xw_hbm, xw_ref), (og_hbm, og_ref))
        )
    ]
    for copy in copies:
        copy.start()
    pad[...] = jnp.zeros_like(pad)
    pad[count : count + 1, :heads] = jnp.exp(alog_ref[...])
    pad[count + 1 : count + 2, :heads] = bias_ref[...]
    copies[0].wait()
    pad[:count, :heads] = mm(in_ref[...], dtw_ref[...], NT)
    rate = pad[count : count + 1, :]
    pre = pad[:count, :] + pad[count + 1 : count + 2, :]
    small = jnp.exp(-jnp.abs(pre))
    delta = jnp.maximum(pre, 0.0) + jnp.log1p(small)
    sig_out[...] = jnp.where(pre >= 0.0, 1.0, small) / (1.0 + small)
    cum = sum_rows(iota((count, count), 0) >= iota((count, count), 1), -rate * delta)
    total = cum[count - 1 : count, :]
    delta_out[...] = delta
    cum_out[...] = cum
    cumt_out[...] = cum.T
    tail = two_terms(delta * jnp.exp(total - cum))
    rise = two_terms(jnp.exp(cum))
    for copy in copies[1:]:
        copy.wait()
    decays = []
    width = 2 * LANES
    for j in range(inner // width):
        span = slice(j * width, (j + 1) * width)
        spread2 = spread_matrix(j * width // HALF, width, 2)
        x = mm(in_ref[...], xw_ref[:, span])
        x_ref[:, span] = x
        xdw_ref[:, span] = (x * mm(tail, spread2)).astype(BF16)
        risen = mm(rise, spread2)
        dye_ref[:, span] = (og_ref[:, span].astype(F32) * risen).astype(BF16)
        decays.append(risen[count - 1 :, :])
    outs = [
        pltpu.make_async_copy(near, far, out_sems.at[n])
        for n, (near, far) in enumerate(((x_ref, x_hbm), (xdw_ref, xdw_hbm), (dye_ref, dye_hbm)))
    ]
    for copy in outs:
        copy.start()
    bc = mm(in_ref[...], bcw_ref[...])
    bc_out[...] = bc
    turned = bc.T
    turned_hi = turned.astype(BF16).astype(F32)
    turned_lo = turned - turned_hi
    b_left = jnp.concatenate([turned_hi[:HALF], turned_lo[:HALF]], axis=0).astype(BF16)
    c_left = jnp.concatenate([turned_hi[HALF:], turned_lo[HALF:]], axis=0).astype(BF16)
    place = lax.axis_index("seq")
    first = lax.rem(place, 2) == 0
    early = place < 4 if lax.axis_size("seq") == 8 else place >= 0
    parts = []
    for j in range(inner // width):
        span = slice(j * width, (j + 1) * width)
        e_part, l_part = mm(b_left, xdw_ref[:, span]), mm(c_left, dye_ref[:, span])
        decay = jnp.broadcast_to(decays[j], (8, width))
        parts.append((e_part[:HALF] + e_part[HALF:], l_part[:HALF] + l_part[HALF:], decay))
    chunks = len(parts)
    for n in range(chunks // 2):
        span = slice(n * width, (n + 1) * width)
        low, high = parts[n], parts[n + chunks // 2]
        e, l, g = (jnp.where(first, one, two) for one, two in zip(low, high))
        mine_out[:HALF, span], mine_out[HALF:LANES, span], mine_out[LANES:, span] = e, l, g
        e, l, g = (jnp.where(first, two, one) for one, two in zip(low, high))
        send1_out[:HALF, span] = jnp.where(early, e, l)
        send1_out[HALF:, span] = g
        send2_out[:, span] = jnp.where(early, l, e)
    for copy in outs:
        copy.wait()


def turn_kernel(in_ref, src_ref, turned_out):
    width = in_ref.shape[1]
    for n in range(turned_out.shape[0]):
        chosen = (iota((width, width), 0) == src_ref[n : n + 1, :]).astype(F32).astype(BF16)
        turned_out[n] = mm(in_ref[...], chosen).T.astype(BF16)


def left_terms(hi, lo):
    low_lanes = iota((1, LANES), 1) < HALF
    first_half = jnp.where(low_lanes, hi, pltpu.roll(lo, HALF, 1))
    return jnp.concatenate([first_half, jnp.where(low_lanes, hi, 0.0)], axis=1).astype(BF16)


def right_terms(hi, lo):
    low_lanes = iota((1, LANES), 1) < HALF
    first_half = jnp.where(low_lanes, hi, pltpu.roll(hi, HALF, 1))
    return jnp.concatenate([first_half, jnp.where(low_lanes, lo, 0.0)], axis=1).astype(BF16)


def quad_kernel(
    part, x_hbm, og_hbm, bc_ref, delta_ref, cum_ref, cumt_ref, skip_ref,
    base_out, dcum_out, dbc_out, direct_out, skip_out,
    x_ref, og_ref, cumx, deltax, skipx, wsum, across, down, scores, pad, prods, sems,
):
    count, width = base_out.shape
    there = pl.ds(part * width, width)
    copies = [
        pltpu.make_async_copy(x_hbm.at[:, there], x_ref, sems.at[0]),
        pltpu.make_async_copy(og_hbm.at[:, there], og_ref, sems.at[1]),
    ]
    for copy in copies:
        copy.start()
    blocks = width // LANES
    heads = skip_ref.shape[1]
    lanes = iota((1, LANES), 1)
    low_lanes = lanes < HALF
    pad[...] = jnp.zeros_like(pad)
    pad[0:1, :heads] = skip_ref[...]
    spread3 = spread_matrix(2 * part * blocks, width, 3)
    cumx[...] = mm(three_terms(cum_ref[...]), spread3)
    deltax[...] = mm(two_terms(delta_ref[...]), spread3[: 2 * LANES])
    skipx[...] = mm(three_terms(pad[...]), spread3)
    bc = bc_ref[...]
    bc_hi = bc.astype(BF16).astype(F32)
    bc_lo = bc - bc_hi
    swapped = pltpu.roll(bc, HALF, 1)
    causal = iota((count, count), 1) >= iota((count, count), 0)
    right = right_terms(pltpu.roll(bc_hi, HALF, 1), pltpu.roll(bc_lo, HALF, 1))
    scores[...] = jnp.where(causal, mm(left_terms(bc_hi, bc_lo), right, NT), 0.0)
    wsum[...] = jnp.zeros_like(wsum)
    across[...] = jnp.zeros_like(across)
    down[...] = jnp.zeros_like(down)
    prods[...] = jnp.zeros_like(prods)
    direct_out[...] = jnp.zeros_like(direct_out)
    starts = list(range(0, count, LANES))
    for copy in copies:
        copy.wait()

    def pair(j, _):
        span = pl.ds(pl.multiple_of(j * LANES, LANES), LANES)
        at = part * blocks + j
        og = og_ref[:, span].astype(F32)
        og_turned = pltpu.roll(og, HALF, 1)
        x_full = x_ref[:, span]
        prods[pl.ds(j, 1), :] = jnp.sum(x_full * og, axis=0, keepdims=True)
        x = x_full * deltax[:, span]
        x_hi = x.astype(BF16).astype(F32)
        x_lo = pltpu.roll(x - x_hi, HALF, 1)
        cumj = cumx[:, span]
        outs = [None] * len(starts)
        for q in range(2):
            mine = low_lanes if q == 0 else jnp.logical_not(low_lanes)
            head = 2 * at + q
            xq = jnp.where(mine, x_hi, x_lo).astype(BF16)
            og_both = jnp.where(mine, og, og_turned).astype(BF16)
            ogq = jnp.where(mine, og, 0.0).astype(BF16)
            row = cumt_ref[pl.ds(head, 1), :]
            row_sum = jnp.zeros((1, count), F32)
            for n, s in enumerate(starts):
                rows = slice(s, s + LANES)
                d = mm(xq[rows], og_both[s:], NT)
                col = cumj[rows, q * HALF : q * HALF + 1]
                a = jnp.exp(jnp.minimum(row[:, s:] - col, 0.0))
                score = scores[rows, s:]
                w = a * d
                wsum[rows, s:] += w
                p = a * score
                p_hi = p.astype(BF16)
                p_lo = (p - p_hi.astype(F32)).astype(BF16)
                z = w * score
                part_sum = jnp.sum(z, axis=0, keepdims=True)
                if s:
                    part_sum = jnp.concatenate([jnp.zeros((1, s), F32), part_sum], axis=1)
                row_sum = row_sum + part_sum
                down[rows, :] += jnp.where(lanes == head, jnp.sum(z, axis=1, keepdims=True), 0.0)
                out = mm(p_hi, ogq[s:]) + mm(p_lo, ogq[s:])
                outs[n] = out if q == 0 else outs[n] + out
            across[pl.ds(head, 1), :] = row_sum
        gather = gather_matrix(2 * at)
        gather2 = jnp.concatenate([gather, gather], axis=0)
        for n, s in enumerate(starts):
            rows = slice(s, s + LANES)
            base_out[rows, span] = deltax[rows, span] * outs[n] + skipx[0:1, span] * og[rows]
            direct_out[rows, :] += mm(two_terms(x_full[rows] * outs[n]), gather2)
        return 0

    lax.fori_loop(0, blocks, pair, 0, unroll=2 if blocks % 2 == 0 else 1)
    dcum_out[...] = across[...].T - down[...]
    wfull = jnp.where(causal, wsum[...], 0.0).astype(BF16)
    swapped = swapped.astype(BF16)
    dbc_out[...] = jnp.where(low_lanes, mm(wfull, swapped), mm(wfull, swapped, TN))
    skip_out[...] = jnp.broadcast_to(head_sums(prods[...], 2 * part * blocks), skip_out.shape)


def close_kernel(
    where_ref, a_mine, a_other, b_mine, b_other, bc_ref, delta_ref, cum_ref, sig_ref, turned_ref,
    alog_ref, x_ref, xdw_ref, dye_ref, *refs,
):
    quads = [refs[5 * n : 5 * n + 5] for n in range(PARTS)]
    dx_out, dbc_out, ddt_out, small_out, *refs = refs[5 * PARTS :]
    sends, (pad, states, falls, rises, prods) = refs[:-5], refs[-5:]
    count, inner = dx_out.shape
    heads = alog_ref.shape[1]
    blocks = inner // LANES
    lanes = iota((1, LANES), 1)
    low_lanes = lanes < HALF
    first, early = where_ref[0] == 0, where_ref[2] == 1
    pad[...] = jnp.zeros_like(pad)
    pad[0:1, :heads] = jnp.exp(alog_ref[...])
    rate = pad[0:1, :]
    prods[...] = jnp.zeros_like(prods)
    delta, cum, bc = delta_ref[...], cum_ref[...], bc_ref[...]
    total = cum[count - 1 : count, :]
    bc_hi = bc.astype(BF16).astype(F32)
    bc_lo = bc - bc_hi
    b_left = left_terms(bc_hi, bc_lo)
    c_left = left_terms(pltpu.roll(bc_hi, HALF, 1), pltpu.roll(bc_lo, HALF, 1))
    fall = jnp.exp(total - cum)
    fall2, tail2 = two_terms(fall), two_terms(delta * fall)
    wide = 2 * LANES
    pad_rows = jnp.zeros((HALF, wide), BF16)
    each = inner // PARTS
    for j in range(inner // wide):
        span = slice(j * wide, (j + 1) * wide)
        base = quads[j * wide // each][0]
        spread = spread_matrix(j * wide // HALF, wide, 2)
        here = slice(j * wide % each, j * wide % each + wide)
        near = slice(j * wide % (inner // 2), j * wide % (inner // 2) + wide)
        lower = j * wide < inner // 2
        one, two = (
            jnp.where(first, mine[:, near], other[:, near])
            if lower
            else jnp.where(first, other[:, near], mine[:, near])
            for mine, other in ((a_mine, a_other), (b_mine, b_other))
        )
        s_state, m_state = jnp.where(early, one, two), jnp.where(early, two, one)
        s_hi, m_hi = s_state.astype(BF16), m_state.astype(BF16)
        s_lo = (s_state - s_hi.astype(F32)).astype(BF16)
        m_lo = (m_state - m_hi.astype(F32)).astype(BF16)
        states[:HALF, span], states[HALF:, span] = m_hi, s_hi
        v1 = mm(b_left, jnp.concatenate([m_hi, m_hi, m_lo, pad_rows], axis=0))
        v2 = mm(c_left, jnp.concatenate([s_hi, s_hi, s_lo, pad_rows], axis=0))
        dx_out[:, span] = (base[:, here] + mm(tail2, spread) * v1).astype(BF16)
        fallen = x_ref[:, span] * (mm(fall2, spread) * v1)
        for kept, value in ((falls, fallen), (rises, dye_ref[:, span].astype(F32) * v2)):
            hi = value.astype(BF16)
            kept[:, span] = hi
            kept[:, inner + j * wide : inner + (j + 1) * wide] = (value - hi.astype(F32)).astype(BF16)
        prod = jnp.sum(s_state * m_state, axis=0, keepdims=True)
        for k in range(wide // LANES):
            at = j * wide // LANES + k
            prods[at : at + 1, :] = prod[:, k * LANES : (k + 1) * LANES]
    row, lane = iota((inner, LANES), 0), iota((inner, LANES), 1)
    gather = (lane == row // HALF).astype(F32).astype(BF16)
    gather = jnp.concatenate([gather, gather], axis=0)
    fallen = mm(falls[...], gather)
    risen = mm(rises[...], gather)
    r1, r2 = mm(xdw_ref[...], states[...], NT), mm(dye_ref[...], states[...], NT)
    dcum, dbcq, direct, skips = (sum(quad[k][...] for quad in quads) for k in range(1, 5))
    dbc_out[...] = (dbcq + jnp.where(low_lanes, r1, r2)).astype(BF16)
    ahead = iota((count, count), 1) - iota((count, count), 0)
    dg = (
        sum_rows(ahead >= 0, dcum + risen)
        + sum_rows(ahead < 0, delta * fallen)
        + jnp.exp(total) * head_sums(prods[...], 0)
    )
    dpre = jnp.where(lanes < heads, (direct + fallen - rate * dg) * sig_ref[...], 0.0)
    dpre_hi = dpre.astype(BF16).astype(F32)
    ddt_out[...] = (dpre_hi + pltpu.roll(dpre - dpre_hi, HALF, 1)).astype(BF16)
    sums = (
        jnp.sum(dg * (-rate) * delta, axis=0, keepdims=True),
        jnp.sum(dpre, axis=0, keepdims=True),
        jnp.where(lanes < heads, skips[0:1], 0.0),
    )
    small = jnp.zeros((8, LANES), F32)
    for n, one in enumerate(sums):
        small = small + pltpu.roll(jnp.broadcast_to(one, (8, LANES)), 32 * (n + 1), 1)
    small_out[...] = small
    weight_part(turned_ref, dx_out, (dbc_out, ddt_out, small_out), sends, True)


def weight_part(turned_ref, dx_ref, more, outs, second):
    rows = turned_ref.shape[1] // 2
    part = slice(rows, 2 * rows) if second else slice(0, rows)
    blocks = dx_ref.shape[1] // LANES
    lanes = iota((1, LANES), 1)
    at = 0
    for n, out in enumerate(outs):
        turned = turned_ref[n, part, :]
        size = out.shape[1] // LANES
        wide = min(at + size, blocks) - at
        if wide > 0:
            out[:, : wide * LANES] = mm(turned, dx_ref[:, at * LANES : (at + wide) * LANES])
        for k in range(max(at, blocks), at + size):
            span = slice((k - at) * LANES, (k - at + 1) * LANES)
            if k == blocks:
                out[:, span] = mm(turned, more[0][...])
            else:
                both = mm(turned, more[1][...])
                both = both + pltpu.roll(both, HALF, 1)
                out[:, span] = jnp.where(lanes < 32, both, more[2][0:1, :])
        at += size


def keep_kernel(turned_ref, dx_ref, dbc_ref, ddt_ref, small_ref, *outs):
    weight_part(turned_ref, dx_ref, (dbc_ref, ddt_ref, small_ref), outs, False)


def grad_kernel(dx_ref, dbc_ref, ddt_ref, xw_ref, bcw_ref, dtw_ref, grad_out, pad):
    heads = dtw_ref.shape[0]
    pad[...] = jnp.zeros_like(pad)
    pad[:heads, :] = dtw_ref[...].astype(F32)
    pad[HALF : HALF + heads, :] = dtw_ref[...].astype(F32)
    grad = mm(dbc_ref[...], bcw_ref[...], NT)
    grad += mm(ddt_ref[...], pad[...].astype(BF16))
    grad += mm(dx_ref[...], xw_ref[...], NT)
    grad_out[...] = grad.astype(BF16)


VMEM = pl.BlockSpec(memory_space=pltpu.VMEM)
SMEM = pl.BlockSpec(memory_space=pltpu.SMEM)


HBM = pl.BlockSpec(memory_space=pltpu.HBM)


def call(kernel, outs, scratch, args, flops, name, specs=None, limit=40, out_specs=None):
    return pl.pallas_call(
        kernel,
        name=name,
        out_shape=[jax.ShapeDtypeStruct(shape, dtype) for shape, dtype in outs],
        in_specs=[(specs or {}).get(n, VMEM) for n in range(len(args))],
        out_specs=[(out_specs or {}).get(n, VMEM) for n in range(len(outs))],
        scratch_shapes=[
            pltpu.VMEM(*one) if isinstance(one, tuple) else one for one in scratch
        ],
        cost_estimate=pl.CostEstimate(
            flops=flops, bytes_accessed=flops // 256, transcendentals=0
        ),
        compiler_params=pltpu.CompilerParams(vmem_limit_bytes=limit * 1024 * 1024),
    )(*args)


def swap(value, axis, bit):
    return lax.ppermute(value, axis, [(k, k ^ bit) for k in range(lax.axis_size(axis))])


def slide(value, axis, step):
    count = lax.axis_size(axis)
    pairs = [(k, k + step) for k in range(count) if 0 <= k + step < count]
    return lax.ppermute(value, axis, pairs)


def swap_by_parity(value, both, k):
    n_dp = lax.axis_size("dp")
    flips = [bit * (n_dp if axis == "seq" else 1) for axis, bit in (order[k] for order in both)]
    pairs = [(n, n ^ flips[n % n_dp % 2]) for n in range(lax.axis_size("seq") * n_dp)]
    return lax.ppermute(value, ("seq", "dp"), pairs)


def bits_of(axis):
    return [(axis, 1 << n) for n in range(lax.axis_size(axis).bit_length() - 1)]


def scans(ahead, behind, decay):
    rows = ahead.shape[0]
    values, passed = [ahead, behind], [jnp.ones_like(decay)] * 2
    totals, decays = [jnp.zeros_like(ahead)] * 2, [decay] * 2
    width, count = 1, lax.axis_size("seq") // 2
    while width < count:
        last = 2 * width >= count
        sent = values
        if not last:
            sent = [jnp.concatenate([v, d], axis=0) for v, d in zip(values, decays)]
        got, _ = yield (
            [functools.partial(slide, v, "seq", 2 * width * d) for v, d in zip(sent, (1, -1))],
            None,
            0,
        )
        for n in range(2):
            new = got[n][:rows]
            totals[n] = totals[n] + passed[n][0:1] * new
            if not last:
                values[n] = values[n] + decays[n][0:1] * new
                passed[n] = passed[n] * got[n][rows:]
                decays[n] = decays[n] * got[n][rows:]
        width *= 2
    return totals


def two_blocks(where_ref, mine_ref, got_ref, logs_ref, early):
    forward = (where_ref[2] == 1) == early
    first = where_ref[0] == 0
    mine, got = jnp.where(forward, mine_ref[:HALF], mine_ref[HALF:LANES]), got_ref[:HALF]
    g_mine, g_got = mine_ref[LANES:], logs_ref[HALF:]
    before, after = jnp.where(first, mine, got), jnp.where(first, got, mine)
    d0, d1 = jnp.where(first, g_mine, g_got), jnp.where(first, g_got, g_mine)
    return forward, before, after, d0, d1


def of_pair(forward, before, after, d0, d1):
    return jnp.where(forward, d1[0:1] * before + after, before + d0[0:1] * after)


def mine_and_other(where_ref, entering, forward, before, after, d0, d1):
    inner = jnp.where(forward, d0[0:1] * entering + before, d1[0:1] * entering + after)
    plain = (where_ref[0] == 0) == forward
    return jnp.where(plain, entering, inner), jnp.where(plain, inner, entering)


def pair_kernel(where_ref, mine_ref, got1_ref, send_out, decay_out):
    blocks = two_blocks(where_ref, mine_ref, got1_ref, got1_ref, True)
    send_out[...] = of_pair(*blocks)
    decay_out[...] = blocks[3] * blocks[4]


def turn_around_kernel(
    where_ref, mine_ref, got1_ref, own_ref, decay_ref, hop1_ref, send_out, mine_out, other_out
):
    entering = hop1_ref[...]
    send_out[...] = own_ref[...] + decay_ref[0:1, :] * entering
    blocks = two_blocks(where_ref, mine_ref, got1_ref, got1_ref, True)
    mine_out[...], other_out[...] = mine_and_other(where_ref, entering, *blocks)


def outward_kernel(where_ref, mine_ref, got1_ref, got2_ref, decay_ref, hop2_ref, send_out):
    blocks = two_blocks(where_ref, mine_ref, got2_ref, got1_ref, False)
    send_out[...] = of_pair(*blocks) + decay_ref[0:1, :] * hop2_ref[...]


def last_kernel(
    where_ref, mine_ref, got1_ref, got2_ref, hop2_ref, hop3_ref, mine_out, other_out
):
    middle = jnp.logical_and(where_ref[1] > 0, where_ref[1] < 3)
    entering = jnp.where(middle, hop2_ref[...], hop3_ref[...])
    blocks = two_blocks(where_ref, mine_ref, got2_ref, got1_ref, False)
    mine_out[...], other_out[...] = mine_and_other(where_ref, entering, *blocks)


def exchange_of_four(mine, send1, send2, where):
    one = (send2.shape, F32)

    def run(kernel, outs, args, name):
        return call(kernel, outs, [], (where, *args), 1_000_000, name, {0: SMEM})

    def across(value):
        return functools.partial(swap, value, "seq", 1)

    def hop(value, *pairs):
        return functools.partial(hop_pairs, value, pairs)

    (got1,), send2 = yield [across(send1)], send2, 0
    own, decay = run(pair_kernel, [one, ((8, mine.shape[1]), F32)], (mine, got1), "pair")
    (hop1, got2), _ = yield [hop(own, (0, 1), (3, 2)), across(send2)], None, 0
    send, a_mine, a_send = run(
        turn_around_kernel, [one] * 3, (mine, got1, own, decay, hop1), "turn_around"
    )
    (hop2, a_other), a_mine = yield [hop(send, (1, 2), (2, 1)), across(a_send)], a_mine, 0
    (send,) = run(outward_kernel, [one], (mine, got1, got2, decay, hop2), "outward")
    (hop3,), _ = yield [hop(send, (1, 0), (2, 3))], None, 0
    b_mine, b_send = run(last_kernel, [one] * 2, (mine, got1, got2, hop2, hop3), "last")
    (b_other,), b_mine = yield [across(b_send)], b_mine, 0
    return a_mine, a_other, b_mine, b_other


def hop_pairs(value, pairs):
    return lax.ppermute(
        value, "seq", [(2 * one + k, 2 * to + k) for one, to in pairs for k in range(2)]
    )


def exchange(mine, send1, send2, first, state):
    (got1, got2), _ = yield (
        [functools.partial(swap, send, "seq", 1) for send in (send1, send2)], None, 0
    )
    got = jnp.concatenate([got1[:state], got2, got1[state:]], axis=0)
    before, after = jnp.where(first, mine, got), jnp.where(first, got, mine)
    e0, l0, g0 = before[:state], before[state : 2 * state], before[2 * state :]
    e1, l1, g1 = after[:state], after[state : 2 * state], after[2 * state :]
    s_in, m_in = yield from scans(
        g1[0:1] * e0 + e1, l0 + g0[0:1] * l1, g0 * g1
    )
    s_second = g0[0:1] * s_in + e0
    m_first = g1[0:1] * m_in + l1
    both_first = jnp.concatenate([m_first, s_in], axis=0)
    both_second = jnp.concatenate([m_in, s_second], axis=0)
    send = jnp.where(first, both_second, both_first)
    mine = jnp.where(first, both_first, both_second)
    (other,), mine = yield [functools.partial(swap, send, "seq", 1)], mine, 0
    return mine[state:], other[state:], mine[:state], other[:state]


def scatter(send, keep, both, holds):
    for k in range(len(both[0])):
        if k:
            size = keep.shape[0] // 2
            send, keep = keep[size:] + got[size:], keep[:size] + got[:size]
        run = functools.partial(swap_by_parity, send, both, k)
        (got,), keep = yield [run], keep, holds.get(k, 0)
    return keep, got


def drive(programs, filled, fillers, token):
    results = [None] * len(programs)
    ready, flying, phase = {n: None for n in range(len(programs))}, {}, 0
    while ready or flying:
        for n in list(ready):
            try:
                runs, more, hold = programs[n].send(ready.pop(n))
                flying[n] = (runs, more, phase + hold)
            except StopIteration as stop:
                results[n] = stop.value
        for n, (runs, more, due) in list(flying.items()):
            flying[n] = ([run() if callable(run) else run for run in runs], more, due)
        extra = {key: run(token) for key, run in fillers.get(phase, ())}
        sent = {n: (runs, more) for n, (runs, more, due) in flying.items() if due <= phase}
        if sent or extra:
            sent, extra, token = lax.optimization_barrier((sent, extra, token))
        for n in sent:
            del flying[n]
        filled.update(extra)
        ready.update(sent)
        phase += 1
    for later in sorted(fillers):
        if later >= phase:
            filled.update({key: run(token) for key, run in fillers[later]})
    return results, token


def body(layer_in, out_grad, x_weight, bc_weight, dt_weight, a_log, dt_bias, skip_gain):
    inner = x_weight.shape[1]
    width = x_weight.shape[0]
    heads = dt_weight.shape[1]
    state = bc_weight.shape[1] // 2
    seq_in, og = layer_in[0], out_grad[0]
    count = seq_in.shape[0]
    tokens_all = count * lax.axis_size("seq") * layer_in.shape[0] * lax.axis_size("dp")
    inv_root = 1.0 / math.sqrt(tokens_all)
    devices = lax.axis_size(("seq", "dp"))
    rows = width // devices
    n_dp = lax.axis_size("dp")
    seq_at, dp_at = lax.axis_index("seq"), lax.axis_index("dp")
    me = seq_at * n_dp + dp_at
    side = (seq_at & 1).astype(jnp.int32)
    early = seq_at < 4 if lax.axis_size("seq") == 8 else seq_at >= 0
    where = jnp.stack([seq_at & 1, seq_at >> 1, early.astype(seq_at.dtype)]).astype(jnp.int32)

    dp_bits, seq_bits = bits_of("dp"), bits_of("seq")
    start, dp_rest = dp_bits[:1], dp_bits[1:]
    y_bit, z_bits = seq_bits[:1], seq_bits[1:]
    orders = [
        (start + dp_rest + y_bit + z_bits, start + y_bit + dp_rest + z_bits[::-1]),
        (
            start + z_bits[:1] + dp_rest + y_bit + z_bits[1:],
            start + z_bits[:1] + y_bit + dp_rest + z_bits[1:],
        ),
    ]
    offsets = np.zeros((2, 8, width), np.int32)
    for n, both in enumerate(orders):
        for parity in range(2):
            for r in range(devices):
                mask = 0
                order = both[parity ^ (r >> (len(both[0]) - 1))]
                for k, (axis, bit) in enumerate(order):
                    if (r >> (len(order) - 1 - k)) & 1:
                        mask ^= bit * (n_dp if axis == "seq" else 1)
                offsets[parity, n, r * rows : (r + 1) * rows] = mask
    offsets = jnp.where((dp_at & 1) == 0, jnp.asarray(offsets[0]), jnp.asarray(offsets[1]))
    within = np.broadcast_to(np.arange(width, dtype=np.int32) % rows, (8, width))
    src = (me ^ offsets) * rows + jnp.asarray(within)

    alog2, bias2, skip2 = (v.reshape(1, heads) for v in (a_log, dt_bias, skip_gain))
    dtw = dt_weight.T
    head_shape = ((count, LANES), F32)
    half, part = inner // 2, inner // PARTS
    first = side == 0
    filled = {}
    mine, send1, send2, bc, delta, cum, cumt, sig, xf, xdw, dye = call(
        first_kernel,
        [((2 * state + 8, half), F32), ((state + 8, half), F32), ((state, half), F32)]
        + [head_shape] * 3 + [((LANES, count), F32), head_shape]
        + [((count, inner), F32)] + [((count, inner), BF16)] * 2,
        [((count + 8, LANES), F32), (seq_in.shape, BF16), (bc_weight.shape, BF16),
         ((count, inner), BF16), ((width, inner), BF16),
         ((count, inner), F32), ((count, inner), BF16), ((count, inner), BF16),
         pltpu.SemaphoreType.DMA((4,)), pltpu.SemaphoreType.DMA((3,))],
        (seq_in, og, x_weight, bc_weight, dtw, alog2, bias2),
        1_000_000_000, "first", {0: HBM, 1: HBM, 2: HBM, 3: HBM}, 60,
        {8: HBM, 9: HBM, 10: HBM},
    )

    def run_turn(_):
        return call(
            turn_kernel, [((len(orders), width, count), BF16)], [], (seq_in, src),
            3_000_000_000, "turn",
        )[0]

    def run_quad(n, og):
        wide = ((count, part), F32)
        return call(
            functools.partial(quad_kernel, n),
            [wide, head_shape, head_shape, head_shape, ((8, LANES), F32)],
            [wide, ((count, part), BF16), wide, wide, ((8, part), F32), ((count, count), F32),
             ((LANES, count), F32), head_shape, ((count, count), F32), ((8, LANES), F32),
             ((16, LANES), F32), pltpu.SemaphoreType.DMA((2,))],
            (xf, og, bc, delta, cum, cumt, skip2),
            4_000_000_000, f"quad{n}", {0: HBM, 1: HBM}, 60,
        )

    ahead = 5 if lax.axis_size("seq") == 8 else 1 + len(seq_bits)
    fillers = {n: [] for n in range(64)}
    for n in range(PARTS):
        fillers[n].append((("quad", n), functools.partial(run_quad, n)))
    fillers[min(3, ahead)].append(("turn", run_turn))
    if lax.axis_size("seq") == 8:
        program = exchange_of_four(mine, send1, send2, where)
    else:
        program = exchange(mine, send1, send2, first, state)
    (states,), og = drive([program], filled, fillers, og)

    shapes = [((width // 2, n * LANES), F32) for n in ROUTES]
    ends = [((count, LANES), BF16)] * 2 + [((8, LANES), F32)]
    turned = filled["turn"]
    args = [where, *states, bc, delta, cum, sig, turned, alog2, xf, xdw, dye]
    for n in range(PARTS):
        args += filled["quad", n]
    dx, dbc, ddt, small, *sends = call(
        close_kernel, [((count, inner), BF16)] + ends + shapes,
        [((8, LANES), F32), ((2 * state, inner), BF16), ((count, 2 * inner), BF16),
         ((count, 2 * inner), BF16), ((16, LANES), F32)],
        args, 1_000_000_000, "close", {0: SMEM},
    )
    keeps = call(keep_kernel, shapes, [], [turned, dx, dbc, ddt, small], 500_000_000, "keep")

    def run_grad(_):
        return call(
            grad_kernel, [((count, width), BF16)], [((LANES, width), F32)],
            [dx, dbc, ddt, x_weight, bc_weight, dtw], 1_000_000_000, "grad",
        )[0]

    programs = [scatter(*both) for both in zip(sends, keeps, orders, HOLDS)][::-1]
    pairs, _ = drive(programs, filled, {GRAD_AT: [("grad", run_grad)]}, og)
    pairs = pairs[::-1]
    blocks = inner // LANES
    pieces, at = {}, 0
    for size, pair in zip(ROUTES, pairs):
        for k in range(size):
            pieces[at + k] = (pair, slice(k * LANES, (k + 1) * LANES))
        at += size

    def total(n):
        (one, new), span = pieces[n]
        return (one[:, span] + new[:, span]) * inv_root

    last = total(blocks + 1)
    return (
        filled["grad"][None],
        jnp.concatenate([total(n) for n in range(blocks)], axis=1),
        total(blocks),
        last[:, :heads],
        last[0, 32 : 32 + heads],
        last[0, 64 : 64 + heads],
        last[0, 96 : 96 + heads],
    )


def solution(mesh):
    return jax.shard_map(
        body,
        mesh=mesh,
        in_specs=(P("dp", "seq", None), P("dp", "seq", None), P(), P(), P(), P(), P(), P()),
        out_specs=(
            P("dp", "seq", None),
            P(("seq", "dp"), None),
            P(("seq", "dp"), None),
            P(("seq", "dp"), None),
            P(),
            P(),
            P(),
        ),
        check_vma=False,
    )
```
